512 devices in a mesh: ctx: 128 (over y, z, core), head: 4 (over x).
Axes of the slice: x: 4, y: 8, z: 8, core: 2. Of those that a mesh axis runs over, the one named last changes fastest.
Arguments:
- queries: bfloat16 [32768, 2048], P('ctx', 'head'), may hold values from -120 to 120
- keys: bfloat16 [32768, 128], P('ctx'), may hold values from -20 to 20
- values: bfloat16 [32768, 128], P('ctx'), may hold values from -6 to 6
- grad_out: bfloat16 [32768, 2048], P('ctx', 'head'), may hold values from -6 to 6
- doc_of_block: int32 [128], replicated, may hold values from 0 to 31, never falling along the last dimension, each value on 1 to 8 neighbouring positions
- pair_list: int32 [128, 7], P('ctx'), may hold values from 0 to 7, as said below
- knock: int32 [16, 128], P('head'), may hold values 0 or 1
Outputs:
- d_queries: bfloat16 [32768, 2048], P('ctx', 'head')
- d_keys: bfloat16 [32768, 128], P('ctx')
- d_values: bfloat16 [32768, 128], P('ctx')
The draws below stay inside these ranges and needn't reach their ends.
Inputs may be any that keep to these rules, and one draw needn't show every extreme that they name: `pair_list`: row b holds distinct offsets from 1 to 7 in its first entries and 0 in the rest; some row holds all 7 offsets; an offset that reaches before block 0 names no block. `doc_of_block`: never falls along the blocks; each document covers 1 to 8 whole blocks, one exactly 8.
All inputs are finite; a program needn't handle non-finite values. No bound on the sum of `knock` on one device may be relied on, other than what follows from the above.
Results may differ from the reference program's by a relative error of at most 0.01.
Values may be sent and summed in bfloat16 or wider, within the bound.
No kernel may reach another device: no remote copies, remote signals or barrier semaphores. Data moves between devices by JAX's collectives and lax.ppermute only.
A program may use at most 128 MiB of HBM per device.

```python
import math
import jax
import jax.numpy as jnp
import numpy as np
from jax import lax

HD = 128
HEADS = 16
Q_DEV = 256
NB = 128
TOKENS = 32768
WIN = 8
DOCS = 32


def query_key_pair(key):
    first, second = jax.random.split(jax.random.fold_in(key, 7), 2)
    base_keys = jnp.clip(jax.random.normal(second, (TOKENS, HD), jnp.float32), -6.0, 6.0)
    base_queries = jnp.clip(jax.random.normal(first, (TOKENS, HEADS * HD), jnp.float32), -6.0, 6.0)
    keys_out = base_keys
    queries_out = base_queries
    return (queries_out, keys_out)


def draw_queries(key, part):
    return query_key_pair(key)[0].astype(jnp.bfloat16)


def draw_keys(key, part):
    return query_key_pair(key)[1].astype(jnp.bfloat16)


def draw_pair_list(key, part):
    first, second, third = jax.random.split(jax.random.fold_in(key, 3), 3)
    spread = WIN - 1
    columns = jnp.arange(spread, dtype=jnp.int32)
    ranks = jax.random.randint(first, (NB, spread), 0, 1 << 20, jnp.int32) * spread + columns[None, :]
    order = jnp.argsort(ranks, axis=1, stable=True).astype(jnp.int32) + 1
    counts = jax.random.randint(second, (NB,), 0, WIN, jnp.int32)
    fullrow = jax.random.randint(third, (), 0, NB, jnp.int32)
    counts = jnp.where(jnp.arange(NB, dtype=jnp.int32) == fullrow, spread, counts)
    return jnp.where(columns[None, :] < counts[:, None], order, 0).astype(jnp.int32)


def set_ends(array, own_key, low, largest):
    extent = array.shape
    spot = [jax.random.randint(jax.random.fold_in(own_key, axis), (), 0, extent[axis]) for axis in range(len(extent))]
    array = array.at[tuple(spot)].set(low)
    longest = extent.index(max(extent))
    spot[longest] = (spot[longest] + 1) % extent[longest]
    return array.at[tuple(spot)].set(largest)


def level_of(own_key, shape, pieces, low, largest):
    gain = 1.0
    for dim, parts in pieces:
        steps = jax.random.uniform(jax.random.fold_in(jax.random.fold_in(own_key, 6), dim), (parts,), jnp.float32, low / len(pieces), largest / len(pieces))
        gain = gain * jnp.repeat(jnp.exp(steps), shape[dim] // parts).reshape((-1,) + (1,) * (len(shape) - 1 - dim))
    return gain


def length_profile(count, total, limit, lean):
    loads = [(1 << 20) // math.isqrt(grade ** lean) + 1 for grade in range(2, count + 1)]
    surplus, given = total - limit - (count - 1), [1] * (count - 1)
    while surplus > 0:
        movable = [i for i in range(count - 1) if given[i] < limit]
        mass, budget = sum([loads[i] for i in movable]), surplus
        for i in movable:
            extra = min(limit - given[i], max(1, budget * loads[i] // mass), surplus)
            given[i] = given[i] + extra
            surplus = surplus - extra
    return np.array([limit] + given)


def uneven_parts(key, number_of, total, most, lean):
    if number_of == 2:
        one = jax.random.randint(key, (), max(1, total - most), min(most, total - 1) + 1)
        return jnp.stack([one, total - one])
    sizes = jnp.asarray(length_profile(number_of, total, most, lean), jnp.int32)
    pairs = (number_of - 1) // 2
    source_of, receiver = sizes[1:1 + 2 * pairs:2], sizes[2:2 + 2 * pairs:2]
    room = jnp.minimum(source_of - 1, most - receiver)
    passed = jax.random.randint(jax.random.fold_in(key, 1), (pairs,), 0, 1 << 20) % (room + 1)
    sizes = sizes.at[1:1 + 2 * pairs:2].set(source_of - passed).at[2:2 + 2 * pairs:2].set(receiver + passed)
    return sizes[jax.random.permutation(jax.random.fold_in(key, 2), number_of)]


def scatter_about(stream_key, shape, scale, reach, cuts=(), kind=jnp.bfloat16):
    level = level_of(stream_key, shape, cuts, -0.22, 0.18) if cuts else 1.0
    entries = jax.random.normal(stream_key, shape, jnp.float32) * scale * level
    return jnp.minimum(jnp.maximum(entries, -reach), reach).astype(kind)


def setup_inputs(seed: int = 0) -> dict:
    arg_keys = jax.random.split(jax.random.key(seed), 8)
    return {
        "queries": draw_queries(jax.random.fold_in(arg_keys[7], 71), 0),
        "keys": draw_keys(jax.random.fold_in(arg_keys[7], 71), 0),
        "values": scatter_about(arg_keys[2], (TOKENS, HD), 1.0, 6.0, ((0, 128),)),
        "grad_out": scatter_about(arg_keys[3], (TOKENS, HEADS * HD), 1.0, 6.0, ((0, 128), (1, 4))),
        "doc_of_block": jnp.searchsorted(jnp.cumsum(uneven_parts(arg_keys[4], DOCS, NB, WIN, 0)), jnp.arange(NB), side="right").astype(jnp.int32),
        "pair_list": draw_pair_list(jax.random.fold_in(arg_keys[7], 71), 0),
        "knock": set_ends((jax.random.randint(arg_keys[6], (HEADS, NB), 0, 4) < 3).astype(jnp.int32), jax.random.fold_in(arg_keys[6], 1), 0, 1),
    }


NEG = -1e30


def reference(queries, keys, values, grad_out, doc_of_block, pair_list, knock):
    scale = HD ** -0.5
    margin = (WIN - 1) * Q_DEV
    span = WIN * Q_DEV
    key_pad = jnp.concatenate([jnp.zeros((margin, HD), jnp.float32), keys.astype(jnp.float32)], axis=0)
    value_pad = jnp.concatenate([jnp.zeros((margin, HD), jnp.float32), values.astype(jnp.float32)], axis=0)
    query_heads = queries.astype(jnp.float32).reshape(TOKENS, HEADS, HD)
    grad_heads = grad_out.astype(jnp.float32).reshape(TOKENS, HEADS, HD)

    def one_block(carry, block):
        key_grads, value_grads = carry
        start = block * Q_DEV
        query_block = lax.dynamic_slice_in_dim(query_heads, start, Q_DEV, 0)
        grad_block = lax.dynamic_slice_in_dim(grad_heads, start, Q_DEV, 0)
        key_window = lax.dynamic_slice_in_dim(key_pad, start, span, 0)
        value_window = lax.dynamic_slice_in_dim(value_pad, start, span, 0)
        position = start - margin + jnp.arange(span, dtype=jnp.int32)
        source = jnp.floor_divide(position, Q_DEV).astype(jnp.int32)
        offset = block - source
        clipped = jnp.clip(source, 0, NB - 1).astype(jnp.int32)
        listed = (offset == 0) | jnp.any(pair_list[block][None, :] == offset[:, None], axis=1)
        same_doc = doc_of_block[clipped] == doc_of_block[block]
        allowed = (position >= 0) & listed & same_doc
        head_keep = (knock[:, clipped] == 1) | (offset == 0)[None, :]
        row_pos = start + jnp.arange(Q_DEV, dtype=jnp.int32)
        causal = position[None, :] <= row_pos[:, None]
        live = allowed[None, None, :] & head_keep[:, None, :] & causal[None, :, :]
        scores = jnp.einsum("ihd,jd->hij", query_block, key_window) * scale
        masked = jnp.where(live, scores, NEG)
        top = jnp.max(masked, axis=2, keepdims=True)
        total = jnp.sum(jnp.exp(masked - top), axis=2, keepdims=True)
        log_total = top + jnp.log(total)
        probs = jnp.exp(masked - log_total)
        grad_probs = jnp.einsum("ihd,jd->hij", grad_block, value_window)
        delta = jnp.sum(probs * grad_probs, axis=2, keepdims=True)
        grad_scores = probs * (grad_probs - delta)
        probs_low = lax.optimization_barrier(probs.astype(jnp.bfloat16)).astype(jnp.float32)
        grad_low = lax.optimization_barrier(grad_scores.astype(jnp.bfloat16)).astype(jnp.float32)
        query_grad = jnp.einsum("hij,jd->ihd", grad_low, key_window) * scale
        key_part = jnp.einsum("hij,ihd->jd", grad_low, query_block) * scale
        value_part = jnp.einsum("hij,ihd->jd", probs_low, grad_block)
        key_grads = lax.dynamic_update_slice_in_dim(
            key_grads, lax.dynamic_slice_in_dim(key_grads, start, span, 0) + key_part, start, 0)
        value_grads = lax.dynamic_update_slice_in_dim(
            value_grads, lax.dynamic_slice_in_dim(value_grads, start, span, 0) + value_part, start, 0)
        return (key_grads, value_grads), query_grad.reshape(Q_DEV, HEADS * HD).astype(jnp.bfloat16)

    zeros = jnp.zeros((margin + TOKENS, HD), jnp.float32)
    (key_grads, value_grads), query_grads = lax.scan(one_block, (zeros, zeros), jnp.arange(NB, dtype=jnp.int32))
    d_queries = query_grads.reshape(TOKENS, HEADS * HD)
    return d_queries, key_grads[margin:].astype(jnp.bfloat16), value_grads[margin:].astype(jnp.bfloat16)
```

```python
import functools

import jax
import jax.numpy as jnp
from jax import lax
from jax.experimental import pallas as pl
from jax.experimental.pallas import tpu as pltpu
from jax.sharding import PartitionSpec as P

NEG = -1e30
BOTH = ("ctx", "head")
NT = (((1,), (1,)), ((), ()))


def attention_kernel(
    info, docs, pairs, knock, q_ref, g_ref, own, same, other, dq_ref, cross_ref, plane_ref, near_ref,
    scores, gprobs, acc, key_t, dq_t, top, total, weighted, last,
):
    rows, width = own.shape[0], own.shape[1] // 2
    heads = q_ref.shape[1] // width
    reach = pairs.shape[1] + 1
    scale = width ** (-0.5)
    here, side = info[0], info[1]
    f32 = jnp.float32

    def block_live(o):
        source = jnp.maximum(here - o, 0)
        listed = functools.reduce(jnp.logical_or, [pairs[0, k] == o for k in range(reach - 1)])
        return (here - o >= 0) & listed & (docs[source] == docs[here])

    lives = [None] + [block_live(o) for o in range(1, reach)]

    def live(o, h):
        return lives[o] & (knock[h, jnp.maximum(here - o, 0)] == 1)

    def tile(o):
        if o == 0:
            return own[...]
        if o % 2 == 0:
            return same[o // 2]
        if o == reach - 1:
            return last[...]
        return other[(o - 1) // 2 + (1 - side)]

    @pl.when(side == 0)
    def _():
        last[...] = same[0]

    @pl.when(side == 1)
    def _():
        last[...] = other[reach // 2 - 1]

    def each(o, h, fn):
        if o == 0:
            fn()
        else:
            pl.when(live(o, h))(fn)

    acc[...] = jnp.zeros_like(acc)
    for o in range(reach):
        def prepare(o=o):
            key_t[o] = tile(o)[:, :width].T
        if o == 0:
            prepare()
        else:
            pl.when(lives[o])(prepare)
    below = lax.broadcasted_iota(jnp.int32, (rows, rows), 0) <= lax.broadcasted_iota(
        jnp.int32, (rows, rows), 1
    )

    for h in range(heads):
        cols = slice(h * width, (h + 1) * width)
        top[...] = jnp.full_like(top, NEG)
        for o in range(reach):
            def first(o=o):
                kv = tile(o)
                s = lax.dot_general(kv[:, :width], q_ref[:, cols], NT, preferred_element_type=f32) * scale
                if o == 0:
                    s = jnp.where(below, s, NEG)
                scores[o] = s
                gprobs[o] = lax.dot_general(kv[:, width:], g_ref[:, cols], NT, preferred_element_type=f32)
                top[...] = jnp.maximum(top[...], jnp.max(s, axis=0, keepdims=True))
            each(o, h, first)
        total[...] = jnp.zeros_like(total)
        weighted[...] = jnp.zeros_like(weighted)
        for o in range(reach):
            def second(o=o):
                e = jnp.exp(scores[o] - top[...])
                scores[o] = e
                total[...] += jnp.sum(e, axis=0, keepdims=True)
                weighted[...] += jnp.sum(e * gprobs[o], axis=0, keepdims=True)
            each(o, h, second)
        inverse = 1.0 / total[...]
        delta = weighted[...] * inverse
        dq_t[...] = jnp.zeros_like(dq_t)
        for o in range(reach):
            def third(o=o):
                p = scores[o] * inverse
                ds = (p * (gprobs[o] - delta)).astype(jnp.bfloat16)
                acc[o, :, :width] += jnp.dot(ds, q_ref[:, cols], preferred_element_type=f32)
                acc[o, :, width:] += jnp.dot(
                    p.astype(jnp.bfloat16), g_ref[:, cols], preferred_element_type=f32
                )
                dq_t[...] += jnp.dot(key_t[o], ds, preferred_element_type=f32)
            each(o, h, third)
        dq_ref[:, cols] = (dq_t[...].T * scale).astype(dq_ref.dtype)

    def term(o):
        return jnp.concatenate([acc[o, :, :width] * scale, acc[o, :, width:]], axis=1)

    near_ref[...] = term(0)
    for o in range(2, reach, 2):
        plane_ref[o // 2] = term(o).astype(plane_ref.dtype)
    for o in range(1, reach - 1, 2):
        cross_ref[(o - 1) // 2 + (1 - side)] = term(o).astype(cross_ref.dtype)

    @pl.when(side == 0)
    def _():
        plane_ref[0] = term(reach - 1).astype(plane_ref.dtype)
        cross_ref[0] = jnp.zeros(cross_ref.shape[1:], cross_ref.dtype)

    @pl.when(side == 1)
    def _():
        cross_ref[reach // 2 - 1] = term(reach - 1).astype(cross_ref.dtype)
        plane_ref[0] = jnp.zeros(plane_ref.shape[1:], plane_ref.dtype)


def plane_pairs(blocks, planes):
    pairs = []
    for block in range(blocks):
        chip, side = block // 2, block % 2
        for plane in range(planes):
            source = 2 * (chip - plane) + side
            if plane == 0:
                source = 2 * (chip - planes) + 1
                if side == 1:
                    continue
            if source >= 0:
                pairs.append((source * planes + plane, block * planes + plane))
    return pairs


def local(queries, keys, values, grad_out, doc_of_block, pair_list, knock):
    rows, width = keys.shape
    heads = queries.shape[1] // width
    reach = pair_list.shape[1] + 1
    blocks = doc_of_block.shape[0]
    planes = lax.axis_size("head")
    here = lax.axis_index("ctx")
    info = jnp.stack([here, here % 2])
    out = plane_pairs(blocks, planes)
    back = [(b, a) for a, b in out]
    swap = [(i, i ^ 1) for i in range(blocks)]
    bf16, f32 = jnp.bfloat16, jnp.float32

    own = jnp.concatenate([keys, values], axis=1)
    fetched = lax.ppermute(own, BOTH, out)
    same = lax.all_to_all(jnp.broadcast_to(fetched, (planes, rows, 2 * width)), "head", 0, 0)
    other = lax.ppermute(jnp.concatenate([own[None], same[1:]], axis=0), "ctx", swap)

    vmem = pl.BlockSpec(memory_space=pltpu.VMEM)
    smem = pl.BlockSpec(memory_space=pltpu.SMEM)
    four = jax.ShapeDtypeStruct((planes, rows, 2 * width), bf16)
    d_queries, cross, plane, near = pl.pallas_call(
        attention_kernel,
        out_shape=(
            jax.ShapeDtypeStruct(queries.shape, bf16),
            four,
            four,
            jax.ShapeDtypeStruct((rows, 2 * width), f32),
        ),
        in_specs=[smem] * 4 + [vmem] * 5,
        out_specs=(vmem,) * 4,
        scratch_shapes=[
            pltpu.VMEM((reach, rows, rows), f32),
            pltpu.VMEM((reach, rows, rows), f32),
            pltpu.VMEM((reach, rows, 2 * width), f32),
            pltpu.VMEM((reach, width, rows), bf16),
            pltpu.VMEM((width, rows), f32),
            pltpu.VMEM((1, rows), f32),
            pltpu.VMEM((1, rows), f32),
            pltpu.VMEM((1, rows), f32),
            pltpu.VMEM((rows, 2 * width), bf16),
        ],
        compiler_params=pltpu.CompilerParams(vmem_limit_bytes=40 << 20),
    )(info, doc_of_block, pair_list, knock, queries, grad_out, own, same, other)

    crossed = lax.ppermute(cross, "ctx", swap).astype(f32)
    summed = jnp.concatenate([plane[:1], (plane[1:] + crossed[1:]).astype(bf16)], axis=0)
    near = near + crossed[0]
    parts = lax.all_to_all(summed, "head", 0, 0)
    sent = jnp.sum(parts.astype(f32), axis=0).astype(bf16)
    landed = lax.ppermute(sent, BOTH, back)
    mine = (landed.astype(f32) + near).astype(bf16)
    every = lax.all_to_all(jnp.broadcast_to(mine, (planes, rows, 2 * width)), "head", 0, 0)
    result = jnp.sum(every.astype(f32), axis=0).astype(bf16)
    return d_queries, result[:, :width], result[:, width:]


def solution(mesh):
    in_specs = (
        P("ctx", "head"),
        P("ctx", None),
        P("ctx", None),
        P("ctx", "head"),
        P(),
        P("ctx", None),
        P("head", None),
    )
    out_specs = (P("ctx", "head"), P("ctx", None), P("ctx", None))
    return jax.shard_map(local, mesh=mesh, in_specs=in_specs, out_specs=out_specs, check_vma=False)
```

```python
import functools

import jax
import jax.numpy as jnp
from jax import lax
from jax.experimental import pallas as pl
from jax.experimental.pallas import tpu as pltpu
from jax.sharding import PartitionSpec as P

NEG = -1e30
BOTH = ("ctx", "head")
NT = (((1,), (1,)), ((), ()))


def attention_kernel(
    info, docs, pairs, knock, q_ref, g_ref, own, same, other, dq_ref, cross_ref, plane_ref, near_ref,
    scores, gprobs, pool, key_t, dq_t, q_all, g_all, probs, grads, count, offset, bias,
):
    rows, width = own.shape[0], own.shape[1] // 2
    heads = q_ref.shape[1] // width
    reach = pairs.shape[1] + 1
    scale = width ** (-0.5)
    here, side = info[0], info[1]
    f32, bf16 = jnp.float32, jnp.bfloat16

    for h in range(heads):
        q_all[h * rows : (h + 1) * rows] = q_ref[:, h * width : (h + 1) * width]
        g_all[h * rows : (h + 1) * rows] = g_ref[:, h * width : (h + 1) * width]

    def admit(o, value):
        slot = count[0]
        pool[slot] = value
        key_t[slot] = value[:, :width].T
        offset[slot] = o
        for h in range(heads):
            kept = 1 if o == 0 else knock[h, jnp.maximum(here - o, 0)]
            bias[slot, h] = jnp.where(kept == 1, 0.0, NEG).astype(f32)
        count[0] = slot + 1

    count[0] = 0
    admit(0, own[...])
    for o in range(1, reach):
        source = jnp.maximum(here - o, 0)
        listed = functools.reduce(jnp.logical_or, [pairs[0, k] == o for k in range(reach - 1)])
        kept = functools.reduce(jnp.logical_or, [knock[h, source] == 1 for h in range(heads)])
        live = (here - o >= 0) & listed & (docs[source] == docs[here]) & kept
        if o % 2 == 0:
            pl.when(live)(lambda o=o: admit(o, same[o // 2]))
        elif o < reach - 1:
            pl.when(live)(lambda o=o: admit(o, other[(o - 1) // 2 + (1 - side)]))
        else:
            pl.when(live & (side == 0))(lambda o=o: admit(o, same[0]))
            pl.when(live & (side == 1))(lambda o=o: admit(o, other[reach // 2 - 1]))
    tiles = count[0]

    below = lax.broadcasted_iota(jnp.int32, (rows, rows), 0) <= lax.broadcasted_iota(
        jnp.int32, (rows, rows), 1
    )
    tops = []
    for h in range(heads):
        part = slice(h * rows, (h + 1) * rows)
        s = lax.dot_general(pool[0, :, :width], q_all[part], NT, preferred_element_type=f32) * scale
        s = jnp.where(below, s, NEG)
        scores[0, :, part] = s
        tops.append(jnp.max(s, axis=0, keepdims=True))

    def first(i, tops):
        fresh = []
        for h in range(heads):
            part = slice(h * rows, (h + 1) * rows)
            s = lax.dot_general(pool[i, :, :width], q_all[part], NT, preferred_element_type=f32)
            s = s * scale + bias[i, h]
            scores[i, :, part] = s
            fresh.append(jnp.maximum(tops[h], jnp.max(s, axis=0, keepdims=True)))
        return tuple(fresh)

    tops = lax.fori_loop(1, tiles, first, tuple(tops))

    def second(i, sums):
        fresh = []
        for h in range(heads):
            part = slice(h * rows, (h + 1) * rows)
            g = lax.dot_general(pool[i, :, width:], g_all[part], NT, preferred_element_type=f32)
            e = jnp.exp(scores[i, :, part] - tops[h])
            gprobs[i, :, part] = g
            scores[i, :, part] = e
            total, weighted = sums[h]
            fresh.append(
                (
                    total + jnp.sum(e, axis=0, keepdims=True),
                    weighted + jnp.sum(e * g, axis=0, keepdims=True),
                )
            )
        return tuple(fresh)

    zero = jnp.zeros((1, rows), f32)
    sums = lax.fori_loop(0, tiles, second, ((zero, zero),) * heads)
    inverse = [1.0 / total for total, _ in sums]
    delta = [weighted * inv for (_, weighted), inv in zip(sums, inverse)]

    def gradients(i):
        for h in range(heads):
            part = slice(h * rows, (h + 1) * rows)
            p = scores[i, :, part] * inverse[h]
            probs[:, part] = p.astype(bf16)
            grads[:, part] = (p * (gprobs[i, :, part] - delta[h])).astype(bf16)
        key_term = jnp.dot(grads[...], q_all[...], preferred_element_type=f32) * scale
        value_term = jnp.dot(probs[...], g_all[...], preferred_element_type=f32)
        query_term = jnp.dot(key_t[i], grads[...], preferred_element_type=f32)
        return key_term, value_term, query_term

    plane_ref[...] = jnp.zeros_like(plane_ref)
    cross_ref[...] = jnp.zeros_like(cross_ref)
    key_term, value_term, query_term = gradients(0)
    near_ref[:, :width] = key_term
    near_ref[:, width:] = value_term
    dq_t[...] = query_term

    def third(i, carry):
        key_term, value_term, query_term = gradients(i)
        dq_t[...] += query_term
        o = offset[i]
        in_plane = (o % 2 == 0) | ((o == reach - 1) & (side == 0))
        plane = jnp.where(o % 2 == 0, o // 2, 0)
        cross = jnp.clip((o - 1) // 2 + (1 - side), 0, reach // 2 - 1)

        @pl.when(in_plane)
        def _():
            plane_ref[plane, :, :width] = key_term.astype(bf16)
            plane_ref[plane, :, width:] = value_term.astype(bf16)

        @pl.when(jnp.logical_not(in_plane))
        def _():
            cross_ref[cross, :, :width] = key_term.astype(bf16)
            cross_ref[cross, :, width:] = value_term.astype(bf16)

        return carry

    lax.fori_loop(1, tiles, third, 0)
    for h in range(heads):
        part = slice(h * rows, (h + 1) * rows)
        dq_ref[:, h * width : (h + 1) * width] = (dq_t[:, part].T * scale).astype(bf16)


def plane_pairs(blocks, planes):
    pairs = []
    for block in range(blocks):
        chip, side = block // 2, block % 2
        for plane in range(planes):
            source = 2 * (chip - plane) + side
            if plane == 0:
                source = 2 * (chip - planes) + 1
                if side == 1:
                    continue
            if source >= 0:
                pairs.append((source * planes + plane, block * planes + plane))
    return pairs


def local(queries, keys, values, grad_out, doc_of_block, pair_list, knock):
    rows, width = keys.shape
    heads = queries.shape[1] // width
    reach = pair_list.shape[1] + 1
    blocks = doc_of_block.shape[0]
    planes = lax.axis_size("head")
    here = lax.axis_index("ctx")
    info = jnp.stack([here, here % 2])
    out = plane_pairs(blocks, planes)
    back = [(b, a) for a, b in out]
    swap = [(i, i ^ 1) for i in range(blocks)]
    bf16, f32 = jnp.bfloat16, jnp.float32

    own = jnp.concatenate([keys, values], axis=1)
    fetched = lax.ppermute(own, BOTH, out)
    same = lax.all_to_all(jnp.broadcast_to(fetched, (planes, rows, 2 * width)), "head", 0, 0)
    other = lax.ppermute(jnp.concatenate([own[None], same[1:]], axis=0), "ctx", swap)

    vmem = pl.BlockSpec(memory_space=pltpu.VMEM)
    smem = pl.BlockSpec(memory_space=pltpu.SMEM)
    four = jax.ShapeDtypeStruct((planes, rows, 2 * width), bf16)
    d_queries, cross, plane, near = pl.pallas_call(
        attention_kernel,
        out_shape=(
            jax.ShapeDtypeStruct(queries.shape, bf16),
            four,
            four,
            jax.ShapeDtypeStruct((rows, 2 * width), f32),
        ),
        in_specs=[smem] * 4 + [vmem] * 5,
        out_specs=(vmem,) * 4,
        scratch_shapes=[
            pltpu.VMEM((reach, rows, heads * rows), f32),
            pltpu.VMEM((reach, rows, heads * rows), f32),
            pltpu.VMEM((reach, rows, 2 * width), bf16),
            pltpu.VMEM((reach, width, rows), bf16),
            pltpu.VMEM((width, heads * rows), f32),
            pltpu.VMEM((heads * rows, width), bf16),
            pltpu.VMEM((heads * rows, width), bf16),
            pltpu.VMEM((rows, heads * rows), bf16),
            pltpu.VMEM((rows, heads * rows), bf16),
            pltpu.SMEM((1,), jnp.int32),
            pltpu.SMEM((reach,), jnp.int32),
            pltpu.SMEM((reach, heads), f32),
        ],
        compiler_params=pltpu.CompilerParams(vmem_limit_bytes=40 << 20),
    )(info, doc_of_block, pair_list, knock, queries, grad_out, own, same, other)

    crossed = lax.ppermute(cross, "ctx", swap).astype(f32)
    summed = jnp.concatenate([plane[:1], (plane[1:] + crossed[1:]).astype(bf16)], axis=0)
    near = near + crossed[0]
    parts = lax.all_to_all(summed, "head", 0, 0)
    sent = jnp.sum(parts.astype(f32), axis=0).astype(bf16)
    landed = lax.ppermute(sent, BOTH, back)
    mine = (landed.astype(f32) + near).astype(bf16)
    every = lax.all_to_all(jnp.broadcast_to(mine, (planes, rows, 2 * width)), "head", 0, 0)
    result = jnp.sum(every.astype(f32), axis=0).astype(bf16)
    return d_queries, result[:, :width], result[:, width:]


def solution(mesh):
    in_specs = (
        P("ctx", "head"),
        P("ctx", None),
        P("ctx", None),
        P("ctx", "head"),
        P(),
        P("ctx", None),
        P("head", None),
    )
    out_specs = (P("ctx", "head"), P("ctx", None), P("ctx", None))
    return jax.shard_map(local, mesh=mesh, in_specs=in_specs, out_specs=out_specs, check_vma=False)
```

```python
import functools

import jax
import jax.numpy as jnp
from jax import lax
from jax.experimental import pallas as pl
from jax.experimental.pallas import tpu as pltpu
from jax.sharding import PartitionSpec as P

NEG = -1e30
BOTH = ("ctx", "head")
NT = (((1,), (1,)), ((), ()))


def list_kernel(info, docs, pairs, pairs2, knock, meta):
    heads, slots = knock.shape[0], (pairs.shape[1] + 1) // 2
    here, side = info[0], info[1]
    for i in range(meta.shape[0]):
        meta[i] = 0
    for d in range(slots + 1):
        block = jnp.maximum(here - 2 * d, 0)
        slot = jnp.clip(jnp.where(side == 0, d, slots - d), 0, slots - 1)
        kept = functools.reduce(jnp.logical_or, [knock[h, block] == 1 for h in range(heads)])
        for which, table in ((0, pairs), (1, pairs2)):
            if which == 0 and d in (0, slots):
                continue
            back = 2 * d + which * (1 - 2 * side)
            query = here + which * (1 - 2 * side)
            listed = functools.reduce(
                jnp.logical_or, [table[0, k] == back for k in range(pairs.shape[1])]
            )
            live = (back > 0) & (here - 2 * d >= 0) & listed & (docs[block] == docs[query]) & kept

            @pl.when(live)
            def _(which=which, block=block, slot=slot):
                entry = (slots - 1) * which + meta[which]
                meta[8 + entry] = slot
                meta[24 + slot] = 1
                for h in range(heads):
                    meta[32 + heads * entry + h] = knock[h, block]
                meta[which] = meta[which] + 1


def first_kernel(q_ref, g_ref, own, exps, gprobs, key_t, stack, stats):
    rows, width = own.shape[0], own.shape[1] // 2
    heads = q_ref.shape[1] // width
    scale = width ** (-0.5)
    f32 = jnp.float32
    for h in range(heads):
        part, cols = slice(h * rows, (h + 1) * rows), slice(h * width, (h + 1) * width)
        stack[0, part], stack[1, part] = q_ref[:, cols], g_ref[:, cols]
    key_t[...] = own[:, :width].T
    stats[...] = jnp.zeros_like(stats)
    below = lax.broadcasted_iota(jnp.int32, (rows, rows), 0) <= lax.broadcasted_iota(
        jnp.int32, (rows, rows), 1
    )
    for h in range(heads):
        part = slice(h * rows, (h + 1) * rows)
        s = lax.dot_general(own[:, :width], stack[0, part], NT, preferred_element_type=f32) * scale
        g = lax.dot_general(own[:, width:], stack[1, part], NT, preferred_element_type=f32)
        s = jnp.where(below, s, NEG)
        top = jnp.max(s, axis=0, keepdims=True)
        e = jnp.exp(s - top)
        exps[:, part] = e
        gprobs[:, part] = g
        stats[0:1, part] = top
        stats[1:2, part] = jnp.sum(e, axis=0, keepdims=True)
        stats[2:3, part] = jnp.sum(e * g, axis=0, keepdims=True)


def scores_kernel(meta, stack, stack2, first_stats, same, exps, gprobs, key_t, stats):
    slots, rows, width = same.shape[0], same.shape[1], same.shape[2] // 2
    span = stack.shape[1]
    heads = span // rows
    scale = width ** (-0.5)
    f32 = jnp.float32

    for slot in range(slots):
        @pl.when(meta[24 + slot] == 1)
        def _(slot=slot):
            key_t[slot] = same[slot, :, :width].T

    stats[...] = jnp.zeros_like(stats)
    for which in range(2):
        stats[which, 0:1] = jnp.full((1, span), NEG, f32)
    stats[0, 3:6] = first_stats[0:3]

    for which, both in ((0, stack), (1, stack2)):
        base = (slots - 1) * which

        def first(i, carry, which=which, both=both, base=base):
            i = base + i
            slot = meta[8 + i]
            for h in range(heads):
                part = slice(h * rows, (h + 1) * rows)
                s = lax.dot_general(
                    same[slot, :, :width], both[0, part], NT, preferred_element_type=f32
                )
                s = s * scale + jnp.where(meta[32 + heads * i + h] == 1, 0.0, NEG).astype(f32)
                exps[i, :, part] = s
                stats[which, 0:1, part] = jnp.maximum(
                    stats[which, 0:1, part], jnp.max(s, axis=0, keepdims=True)
                )
            return carry

        def second(i, carry, which=which, both=both, base=base):
            i = base + i
            slot = meta[8 + i]
            for h in range(heads):
                part = slice(h * rows, (h + 1) * rows)
                g = lax.dot_general(
                    same[slot, :, width:], both[1, part], NT, preferred_element_type=f32
                )
                e = jnp.exp(exps[i, :, part] - stats[which, 0:1, part])
                gprobs[i, :, part] = g
                exps[i, :, part] = e
                stats[which, 1:2, part] += jnp.sum(e, axis=0, keepdims=True)
                stats[which, 2:3, part] += jnp.sum(e * g, axis=0, keepdims=True)
            return carry

        lax.fori_loop(0, meta[which], first, 0)
        lax.fori_loop(0, meta[which], second, 0)


def terms_kernel(
    info, meta, first_exps, first_gprobs, first_key_t, exps, gprobs, key_t, stack, stack2, mine, theirs,
    plane_ref, near_ref, dq_ref, factors, acc, probs, grads,
):
    rows, width = key_t.shape[2], key_t.shape[1]
    span = stack.shape[1]
    slots = plane_ref.shape[0]
    scale = width ** (-0.5)
    side = info[1]
    stacks = (stack, stack2)
    f32, bf16 = jnp.float32, jnp.bfloat16

    def three(ref, which, row):
        return ref[which, row : row + 1], ref[which, row + 1 : row + 2], ref[which, row + 2 : row + 3]

    groups = (
        (three(mine, 0, 0), three(mine, 0, 3), three(theirs, 1, 0)),
        (three(mine, 1, 0), three(theirs, 0, 0), three(theirs, 0, 3)),
    )
    for which, group in enumerate(groups):
        high = functools.reduce(jnp.maximum, [top for top, _, _ in group])
        shares = [jnp.exp(top - high) for top, _, _ in group]
        total = sum(share * part for share, (_, part, _) in zip(shares, group))
        weighted = sum(share * part for share, (_, _, part) in zip(shares, group))
        inverse = 1.0 / total
        factors[which, 0:1] = shares[0] * inverse
        factors[which, 1:2] = weighted * inverse
        factors[which, 2:3] = shares[1] * inverse

    def gradients(load_e, load_g, keys, which, row):
        for h in range(span // rows):
            part = slice(h * rows, (h + 1) * rows)
            p = load_e(part) * factors[which, row : row + 1, part]
            probs[:, part] = p.astype(bf16)
            grads[:, part] = (p * (load_g(part) - factors[which, 1:2, part])).astype(bf16)
        key_term = jnp.dot(grads[...], stacks[which][0], preferred_element_type=f32) * scale
        value_term = jnp.dot(probs[...], stacks[which][1], preferred_element_type=f32)
        query_term = jnp.dot(keys, grads[...], preferred_element_type=f32)
        return key_term, value_term, query_term

    acc[...] = jnp.zeros_like(acc)
    key_term, value_term, query_term = gradients(
        lambda part: first_exps[:, part], lambda part: first_gprobs[:, part], first_key_t[...], 0, 2
    )
    near_ref[:, :width] = key_term
    near_ref[:, width:] = value_term
    dq_ref[0] = query_term
    dq_ref[1] = jnp.zeros_like(query_term)

    for which in range(2):
        def step(i, carry, which=which):
            i = (slots - 1) * which + i
            slot = meta[8 + i]
            key_term, value_term, query_term = gradients(
                lambda part: exps[i, :, part], lambda part: gprobs[i, :, part], key_t[slot], which, 0
            )
            acc[slot, :, :width] += key_term
            acc[slot, :, width:] += value_term
            dq_ref[which] += query_term
            return carry

        lax.fori_loop(0, meta[which], step, 0)
    for slot in range(1, slots):
        plane_ref[slot] = acc[slot].astype(bf16)

    @pl.when(side == 0)
    def _():
        near_ref[...] += acc[0]
        plane_ref[0] = jnp.zeros(plane_ref.shape[1:], bf16)

    @pl.when(side == 1)
    def _():
        plane_ref[0] = acc[0].astype(bf16)


def queries_kernel(mine, theirs, dq_ref):
    width, rows = mine.shape[1], dq_ref.shape[0]
    scale = width ** (-0.5)
    for h in range(dq_ref.shape[1] // width):
        part = slice(h * rows, (h + 1) * rows)
        dq = (mine[0, :, part] + theirs[:, part]) * scale
        dq_ref[:, h * width : (h + 1) * width] = dq.T.astype(dq_ref.dtype)


def plane_pairs(blocks, planes):
    pairs = []
    for block in range(blocks):
        for plane in range(planes):
            source = block - 2 * (plane if block % 2 == 0 else planes - plane)
            if source >= 0:
                pairs.append((source * planes + plane, block * planes + plane))
    return pairs


def local(queries, keys, values, grad_out, doc_of_block, pair_list, knock):
    rows, width = keys.shape
    heads = queries.shape[1] // width
    reach = pair_list.shape[1] + 1
    blocks = doc_of_block.shape[0]
    planes = lax.axis_size("head")
    here = lax.axis_index("ctx")
    info = jnp.stack([here, here % 2])
    out = plane_pairs(blocks, planes)
    back = [(b, a) for a, b in out if a != b]
    swap = [(i, i ^ 1) for i in range(blocks)]
    bf16, f32 = jnp.bfloat16, jnp.float32
    span = heads * rows

    edge = jnp.zeros((), bf16)
    own = lax.pad(keys, edge, ((0, 0, 0), (0, width, 0))) + lax.pad(values, edge, ((0, 0, 0), (width, 0, 0)))
    fetched = lax.ppermute(own, BOTH, out)
    pairs2 = lax.ppermute(pair_list, "ctx", swap)

    vmem = pl.BlockSpec(memory_space=pltpu.VMEM)
    smem = pl.BlockSpec(memory_space=pltpu.SMEM)
    params = pltpu.CompilerParams(vmem_limit_bytes=20 << 20)
    meta = pl.pallas_call(
        list_kernel,
        out_shape=jax.ShapeDtypeStruct((32 + heads * reach,), jnp.int32),
        in_specs=[smem] * 5,
        out_specs=smem,
        compiler_params=params,
    )(info, doc_of_block, pair_list, pairs2, knock)
    exps0, gprobs0, key0_t, stack, stats0 = pl.pallas_call(
        first_kernel,
        out_shape=(
            pltpu.VMEM((rows, span), f32),
            pltpu.VMEM((rows, span), f32),
            pltpu.VMEM((width, rows), bf16),
            jax.ShapeDtypeStruct((2, span, width), bf16),
            jax.ShapeDtypeStruct((8, span), f32),
        ),
        in_specs=[vmem] * 3,
        out_specs=(vmem,) * 5,
        compiler_params=params,
    )(queries, grad_out, own)
    stack2 = lax.ppermute(stack, "ctx", swap)
    fetched, stats0, meta = lax.optimization_barrier((fetched, stats0, meta))
    same = lax.all_to_all(jnp.broadcast_to(fetched, (planes, rows, 2 * width)), "head", 0, 0)
    exps, gprobs, key_t, mine = pl.pallas_call(
        scores_kernel,
        out_shape=(
            pltpu.VMEM((reach - 1, rows, span), f32),
            pltpu.VMEM((reach - 1, rows, span), f32),
            pltpu.VMEM((planes, width, rows), bf16),
            jax.ShapeDtypeStruct((2, 8, span), f32),
        ),
        in_specs=[smem] + [vmem] * 4,
        out_specs=(vmem,) * 4,
        compiler_params=params,
    )(meta, stack, stack2, stats0, same)
    theirs = lax.ppermute(mine, "ctx", swap)
    plane, near, dq = pl.pallas_call(
        terms_kernel,
        out_shape=(
            jax.ShapeDtypeStruct((planes, rows, 2 * width), bf16),
            jax.ShapeDtypeStruct((rows, 2 * width), f32),
            jax.ShapeDtypeStruct((2, width, span), f32),
        ),
        in_specs=[smem] * 2 + [vmem] * 10,
        out_specs=(vmem,) * 3,
        scratch_shapes=[
            pltpu.VMEM((2, 8, span), f32),
            pltpu.VMEM((planes, rows, 2 * width), f32),
            pltpu.VMEM((rows, span), bf16),
            pltpu.VMEM((rows, span), bf16),
        ],
        compiler_params=params,
    )(info, meta, exps0, gprobs0, key0_t, exps, gprobs, key_t, stack, stack2, mine, theirs)

    parts = lax.all_to_all(plane, "head", 0, 0)
    sent = jnp.sum(parts.astype(f32), axis=0).astype(bf16)
    landed = lax.ppermute(sent, BOTH, back)
    dq2 = lax.ppermute(dq[1], "ctx", swap)
    d_queries = pl.pallas_call(
        queries_kernel,
        out_shape=jax.ShapeDtypeStruct(queries.shape, bf16),
        in_specs=[vmem] * 2,
        out_specs=vmem,
    )(dq, dq2)
    mine = (landed.astype(f32) + near).astype(bf16)
    every = lax.all_to_all(jnp.broadcast_to(mine, (planes, rows, 2 * width)), "head", 0, 0)
    result = jnp.sum(every.astype(f32), axis=0).astype(bf16)
    return d_queries, result[:, :width], result[:, width:]


def solution(mesh):
    in_specs = (
        P("ctx", "head"),
        P("ctx", None),
        P("ctx", None),
        P("ctx", "head"),
        P(),
        P("ctx", None),
        P("head", None),
    )
    out_specs = (P("ctx", "head"), P("ctx", None), P("ctx", None))
    return jax.shard_map(local, mesh=mesh, in_specs=in_specs, out_specs=out_specs, check_vma=False)
```

```python
import functools

import jax
import jax.numpy as jnp
from jax import lax
from jax.experimental import pallas as pl
from jax.experimental.pallas import tpu as pltpu
from jax.sharding import PartitionSpec as P

NEG = -1e30
BOTH = ("ctx", "head")
NT = (((1,), (1,)), ((), ()))
GRANT = 12


KEEP, OTHER = 8, 24


def list_kernel(info, docs, pairs, knock, early):
    heads, slots = knock.shape[0], (pairs.shape[1] + 1) // 2
    here, side = info[0], info[1]
    early[0] = 0
    for d in range(slots + 1):
        block = jnp.maximum(here - 2 * d, 0)
        kept = functools.reduce(jnp.logical_or, [knock[h, block] == 1 for h in range(heads)])
        kept = kept & (here - 2 * d >= 0)
        back = 2 * d + 1 - 2 * side
        query = here + 1 - 2 * side
        candidate = (back > 0) & (back < 2 * slots) & kept & (docs[block] == docs[query])
        early[OTHER + d] = jnp.where(candidate, 1, 0)
        for h in range(heads):
            early[32 + heads * d + h] = knock[h, block]
        if 0 < d < slots:
            listed = functools.reduce(
                jnp.logical_or, [pairs[0, k] == 2 * d for k in range(pairs.shape[1])]
            )

            @pl.when(kept & listed & (docs[block] == docs[here]))
            def _(d=d, block=block):
                entry = early[0]
                early[1 + entry] = jnp.where(side == 0, d, slots - d)
                for h in range(heads):
                    early[KEEP + heads * entry + h] = knock[h, block]
                early[0] = entry + 1


def first_kernel(q_ref, g_ref, own, pairs, exps, gprobs, key_t, stack, stats):
    rows, width = own.shape[0], own.shape[1] // 2
    heads = q_ref.shape[1] // width
    span = heads * rows
    scale = width ** (-0.5)
    f32 = jnp.float32

    for h in range(heads):
        part, cols = slice(h * rows, (h + 1) * rows), slice(h * width, (h + 1) * width)
        stack[h * rows : (h + 1) * rows] = q_ref[:, cols]
        stack[span + h * rows : span + (h + 1) * rows] = g_ref[:, cols]
    stack[2 * span :] = jnp.zeros((16, width), stack.dtype)
    listed = jnp.broadcast_to(pairs[...].astype(f32), (16, pairs.shape[1]))
    stack[2 * span :, : pairs.shape[1]] = listed.astype(stack.dtype)
    key_t[...] = own[:, :width].T
    stats[...] = jnp.zeros_like(stats)
    below = lax.broadcasted_iota(jnp.int32, (rows, rows), 0) <= lax.broadcasted_iota(
        jnp.int32, (rows, rows), 1
    )
    for h in range(heads):
        part, cols = slice(h * rows, (h + 1) * rows), slice(h * width, (h + 1) * width)
        s = lax.dot_general(own[:, :width], q_ref[:, cols], NT, preferred_element_type=f32) * scale
        g = lax.dot_general(own[:, width:], g_ref[:, cols], NT, preferred_element_type=f32)
        s = jnp.where(below, s, NEG)
        top = jnp.max(s, axis=0, keepdims=True)
        e = jnp.exp(s - top)
        exps[:, part] = e
        gprobs[:, part] = g
        stats[0:1, part] = top
        stats[1:2, part] = jnp.sum(e, axis=0, keepdims=True)
        stats[2:3, part] = jnp.sum(e * g, axis=0, keepdims=True)


def scores_kernel(info, early, stack, stack2, first_stats, same, exps, gprobs, key_t, stats, late):
    slots, rows, width = same.shape[0], same.shape[1], same.shape[2] // 2
    span = (stack.shape[0] - 16) // 2
    heads = span // rows
    scale = width ** (-0.5)
    side = info[1]
    f32 = jnp.float32

    table = stack2[2 * span :].astype(f32)[0:1]
    bits = jnp.zeros_like(table)
    for d in range(slots + 1):
        back = 2 * d + 1 - 2 * side
        match = (table == back.astype(f32)) & (back > 0)
        bits = bits + jnp.where(match, float(1 << d), 0.0)
    bits = jnp.sum(bits).astype(jnp.int32)
    late[0] = 0
    for d in range(slots + 1):
        @pl.when((early[OTHER + d] == 1) & (((bits >> d) & 1) == 1))
        def _(d=d):
            entry = late[0]
            late[1 + entry] = jnp.where(side == 0, d, slots - d)
            for h in range(heads):
                late[KEEP + heads * entry + h] = early[32 + heads * d + h]
            late[0] = entry + 1

    stats[...] = jnp.zeros_like(stats)
    for which in range(2):
        stats[which, 0:1] = jnp.full((1, span), NEG, f32)
    stats[0, 3:6] = first_stats[0:3]

    for which, both, meta in ((0, stack, early), (1, stack2, late)):
        base = (slots - 1) * which

        def first(k, carry, which=which, both=both, base=base, meta=meta):
            i, slot = base + k, meta[1 + k]
            key_t[slot] = same[slot, :, :width].T
            for h in range(heads):
                part = slice(h * rows, (h + 1) * rows)
                s = lax.dot_general(
                    same[slot, :, :width], both[part], NT, preferred_element_type=f32
                )
                s = s * scale + jnp.where(meta[KEEP + heads * k + h] == 1, 0.0, NEG).astype(f32)
                exps[i, :, part] = s
                stats[which, 0:1, part] = jnp.maximum(
                    stats[which, 0:1, part], jnp.max(s, axis=0, keepdims=True)
                )
            return carry

        def second(k, carry, which=which, both=both, base=base, meta=meta):
            i, slot = base + k, meta[1 + k]
            for h in range(heads):
                part = slice(h * rows, (h + 1) * rows)
                g = lax.dot_general(
                    same[slot, :, width:], both[span + h * rows : span + (h + 1) * rows], NT, preferred_element_type=f32
                )
                e = jnp.exp(exps[i, :, part] - stats[which, 0:1, part])
                gprobs[i, :, part] = g
                exps[i, :, part] = e
                stats[which, 1:2, part] += jnp.sum(e, axis=0, keepdims=True)
                stats[which, 2:3, part] += jnp.sum(e * g, axis=0, keepdims=True)
            return carry

        lax.fori_loop(0, meta[0], first, 0)
        lax.fori_loop(0, meta[0], second, 0)


def terms_kernel(
    info, early, late, first_exps, first_gprobs, first_key_t, exps, gprobs, key_t, stack, stack2, mine, theirs,
    plane_ref, near_ref, dq_ref, factors, acc, probs, grads,
):
    rows, width = exps.shape[1], stack.shape[1]
    span = exps.shape[2]
    slots = plane_ref.shape[0]
    scale = width ** (-0.5)
    side = info[1]
    stacks = (stack, stack2)
    f32, bf16 = jnp.float32, jnp.bfloat16

    def three(ref, which, row):
        return ref[which, row : row + 1], ref[which, row + 1 : row + 2], ref[which, row + 2 : row + 3]

    groups = (
        (three(mine, 0, 0), three(mine, 0, 3), three(theirs, 1, 0)),
        (three(mine, 1, 0), three(theirs, 0, 0), three(theirs, 0, 3)),
    )
    for which, group in enumerate(groups):
        high = functools.reduce(jnp.maximum, [top for top, _, _ in group])
        shares = [jnp.exp(top - high) for top, _, _ in group]
        total = sum(share * part for share, (_, part, _) in zip(shares, group))
        weighted = sum(share * part for share, (_, _, part) in zip(shares, group))
        inverse = 1.0 / total
        factors[which, 0:1] = shares[0] * inverse
        factors[which, 1:2] = weighted * inverse
        factors[which, 2:3] = shares[1] * inverse

    def gradients(load_e, load_g, keys, which, row):
        for h in range(span // rows):
            part = slice(h * rows, (h + 1) * rows)
            p = load_e(part) * factors[which, row : row + 1, part]
            probs[:, part] = p.astype(bf16)
            grads[:, part] = (p * (load_g(part) - factors[which, 1:2, part])).astype(bf16)
        key_term = jnp.dot(grads[...], stacks[which][:span], preferred_element_type=f32) * scale
        value_term = jnp.dot(probs[...], stacks[which][span : 2 * span], preferred_element_type=f32)
        return key_term, value_term, jnp.dot(keys, grads[...], preferred_element_type=f32)

    acc[...] = jnp.zeros_like(acc)
    key_term, value_term, dq_ref[0] = gradients(
        lambda part: first_exps[:, part], lambda part: first_gprobs[:, part], first_key_t[...], 0, 2
    )
    dq_ref[1] = jnp.zeros(dq_ref.shape[1:], f32)
    near_ref[:, :width] = key_term
    near_ref[:, width:] = value_term

    for which, meta in ((0, early), (1, late)):
        def step(k, carry, which=which, meta=meta):
            i, slot = (slots - 1) * which + k, meta[1 + k]
            key_term, value_term, query_term = gradients(
                lambda part: exps[i, :, part], lambda part: gprobs[i, :, part], key_t[slot], which, 0
            )
            dq_ref[which] += query_term
            acc[slot, :, :width] += key_term
            acc[slot, :, width:] += value_term
            return carry

        lax.fori_loop(0, meta[0], step, 0)
    for slot in range(1, slots):
        plane_ref[slot] = acc[slot].astype(bf16)

    @pl.when(side == 0)
    def _():
        near_ref[...] += acc[0]
        plane_ref[0] = jnp.zeros(plane_ref.shape[1:], bf16)

    @pl.when(side == 1)
    def _():
        plane_ref[0] = acc[0].astype(bf16)


def queries_kernel(mine, theirs, dq_ref):
    width, rows = mine.shape[1], dq_ref.shape[0]
    scale = width ** (-0.5)
    for h in range(dq_ref.shape[1] // width):
        part = slice(h * rows, (h + 1) * rows)
        dq = (mine[0, :, part] + theirs[:, part]) * scale
        dq_ref[:, h * width : (h + 1) * width] = dq.T.astype(dq_ref.dtype)


def plane_pairs(blocks, planes):
    pairs = []
    for block in range(blocks):
        for plane in range(planes):
            source = block - 2 * (plane if block % 2 == 0 else planes - plane)
            if source >= 0:
                pairs.append((source * planes + plane, block * planes + plane))
    return pairs


def local(queries, keys, values, grad_out, doc_of_block, pair_list, knock):
    rows, width = keys.shape
    heads = queries.shape[1] // width
    reach = pair_list.shape[1] + 1
    blocks = doc_of_block.shape[0]
    planes = lax.axis_size("head")
    here = lax.axis_index("ctx")
    info = jnp.stack([here, here % 2])
    out = plane_pairs(blocks, planes)
    back = [(b, a) for a, b in out if a != b]
    swap = [(i, i ^ 1) for i in range(blocks)]
    bf16, f32 = jnp.bfloat16, jnp.float32
    span = heads * rows

    edge = jnp.zeros((), bf16)
    own = lax.pad(keys, edge, ((0, 0, 0), (0, width, 0))) + lax.pad(values, edge, ((0, 0, 0), (width, 0, 0)))
    fetched = lax.ppermute(own, BOTH, out)
    vmem = pl.BlockSpec(memory_space=pltpu.VMEM)
    smem = pl.BlockSpec(memory_space=pltpu.SMEM)

    def grant(mebibytes):
        return pltpu.CompilerParams(vmem_limit_bytes=mebibytes << 20)

    work = pl.CostEstimate(flops=10**10, bytes_accessed=1 << 22, transcendentals=0)
    lists = jax.ShapeDtypeStruct((32 + heads * (planes + 1),), jnp.int32)
    early = pl.pallas_call(
        list_kernel,
        out_shape=lists,
        in_specs=[smem] * 4,
        out_specs=smem,
        compiler_params=grant(GRANT),
        cost_estimate=work,
    )(info, doc_of_block, pair_list, knock)
    exps0, gprobs0, key0_t, stack, stats0 = pl.pallas_call(
        first_kernel,
        out_shape=(
            pltpu.VMEM((rows, span), f32),
            pltpu.VMEM((rows, span), f32),
            pltpu.VMEM((width, rows), bf16),
            jax.ShapeDtypeStruct((2 * span + 16, width), bf16),
            jax.ShapeDtypeStruct((8, span), f32),
        ),
        in_specs=[vmem] * 4,
        out_specs=(vmem,) * 5,
        compiler_params=grant(GRANT),
        cost_estimate=work,
    )(queries, grad_out, own, pair_list)
    stack2 = lax.ppermute(stack, "ctx", swap)
    fetched, stats0, early = lax.optimization_barrier((fetched, stats0, early))
    same = lax.all_to_all(jnp.broadcast_to(fetched, (planes, rows, 2 * width)), "head", 0, 0)
    exps, gprobs, key_t, mine, late = pl.pallas_call(
        scores_kernel,
        out_shape=(
            pltpu.VMEM((reach - 1, rows, span), f32),
            pltpu.VMEM((reach - 1, rows, span), f32),
            pltpu.VMEM((planes, width, rows), bf16),
            jax.ShapeDtypeStruct((2, 8, span), f32),
            lists,
        ),
        in_specs=[smem] * 2 + [vmem] * 4,
        out_specs=(vmem,) * 4 + (smem,),
        compiler_params=grant(GRANT),
    )(info, early, stack, stack2, stats0, same)
    theirs = lax.ppermute(mine, "ctx", swap)
    plane, near, dq = pl.pallas_call(
        terms_kernel,
        out_shape=(
            jax.ShapeDtypeStruct((planes, rows, 2 * width), bf16),
            jax.ShapeDtypeStruct((rows, 2 * width), f32),
            jax.ShapeDtypeStruct((2, width, span), f32),
        ),
        in_specs=[smem] * 3 + [vmem] * 10,
        out_specs=(vmem,) * 3,
        scratch_shapes=[
            pltpu.VMEM((2, 8, span), f32),
            pltpu.VMEM((planes, rows, 2 * width), f32),
            pltpu.VMEM((rows, span), bf16),
            pltpu.VMEM((rows, span), bf16),
        ],
        compiler_params=grant(GRANT),
    )(info, early, late, exps0, gprobs0, key0_t, exps, gprobs, key_t, stack, stack2, mine, theirs)

    parts = lax.all_to_all(plane, "head", 0, 0)
    sent = jnp.sum(parts.astype(f32), axis=0).astype(bf16)
    landed = lax.ppermute(sent, BOTH, back)
    dq2 = lax.ppermute(dq[1], "ctx", swap)
    d_queries = pl.pallas_call(
        queries_kernel,
        out_shape=jax.ShapeDtypeStruct(queries.shape, bf16),
        in_specs=[vmem] * 2,
        out_specs=vmem,
    )(dq, dq2)
    mine = (landed.astype(f32) + near).astype(bf16)
    every = lax.all_to_all(jnp.broadcast_to(mine, (planes, rows, 2 * width)), "head", 0, 0)
    d_keys = sum(every[i, :, :width].astype(f32) for i in range(planes)).astype(bf16)
    d_values = sum(every[i, :, width:].astype(f32) for i in range(planes)).astype(bf16)
    return d_queries, d_keys, d_values


def solution(mesh):
    in_specs = (
        P("ctx", "head"),
        P("ctx", None),
        P("ctx", None),
        P("ctx", "head"),
        P(),
        P("ctx", None),
        P("head", None),
    )
    out_specs = (P("ctx", "head"), P("ctx", None), P("ctx", None))
    return jax.shard_map(local, mesh=mesh, in_specs=in_specs, out_specs=out_specs, check_vma=False)
```

```python
import functools

import jax
import jax.numpy as jnp
from jax import lax
from jax.experimental import pallas as pl
from jax.experimental.pallas import tpu as pltpu
from jax.sharding import PartitionSpec as P

NEG = -1e30
BOTH = ("ctx", "head")
NT = (((1,), (1,)), ((), ()))
GRANT = 12


KEEP, OTHER, SIDE = 8, 24, 30


def list_kernel(info, docs, pairs, knock, early):
    heads, slots = knock.shape[0], (pairs.shape[1] + 1) // 2
    here, side = info[0], info[1]
    early[0] = 0
    early[SIDE] = side
    for d in range(slots + 1):
        block = jnp.maximum(here - 2 * d, 0)
        kept = functools.reduce(jnp.logical_or, [knock[h, block] == 1 for h in range(heads)])
        kept = kept & (here - 2 * d >= 0)
        back = 2 * d + 1 - 2 * side
        query = here + 1 - 2 * side
        candidate = (back > 0) & (back < 2 * slots) & kept & (docs[block] == docs[query])
        early[OTHER + d] = jnp.where(candidate, 1, 0)
        for h in range(heads):
            early[32 + heads * d + h] = knock[h, block]
        if 0 < d < slots:
            listed = functools.reduce(
                jnp.logical_or, [pairs[0, k] == 2 * d for k in range(pairs.shape[1])]
            )

            @pl.when(kept & listed & (docs[block] == docs[here]))
            def _(d=d, block=block):
                entry = early[0]
                early[1 + entry] = jnp.where(side == 0, d, slots - d)
                for h in range(heads):
                    early[KEEP + heads * entry + h] = knock[h, block]
                early[0] = entry + 1


def first_kernel(q_ref, g_ref, own, pairs, both, key_t, stack, stats, arrivals):
    rows, width = own.shape[0], own.shape[1] // 2
    heads = q_ref.shape[1] // width
    span = heads * rows
    scale = width ** (-0.5)
    f32 = jnp.float32

    copies = []
    for n, source in enumerate((q_ref, g_ref)):
        for h in range(heads):
            place = n * span + h * rows
            copy = pltpu.make_async_copy(
                source.at[:, pl.ds(h * width, width)],
                stack.at[pl.ds(place, rows)],
                arrivals.at[n * heads + h],
            )
            copy.start()
            copies.append(copy)
    stack[2 * span :] = jnp.zeros((16, width), stack.dtype)
    listed = jnp.broadcast_to(pairs[...].astype(f32), (16, pairs.shape[1]))
    stack[2 * span :, : pairs.shape[1]] = listed.astype(stack.dtype)
    key_t[...] = own[:, :width].T
    stats[...] = jnp.zeros_like(stats)
    below = lax.broadcasted_iota(jnp.int32, (rows, rows), 0) <= lax.broadcasted_iota(
        jnp.int32, (rows, rows), 1
    )
    for copy in copies:
        copy.wait()
    for h in range(heads):
        part = slice(h * rows, (h + 1) * rows)
        late_part = slice(span + h * rows, span + (h + 1) * rows)
        s = lax.dot_general(own[:, :width], stack[part], NT, preferred_element_type=f32) * scale
        g = lax.dot_general(own[:, width:], stack[late_part], NT, preferred_element_type=f32)
        s = jnp.where(below, s, NEG)
        top = jnp.max(s, axis=0, keepdims=True)
        e = jnp.exp(s - top)
        both[0, :, part] = e
        both[1, :, part] = g
        stats[0:1, part] = top
        stats[1:2, part] = jnp.sum(e, axis=0, keepdims=True)
        stats[2:3, part] = jnp.sum(e * g, axis=0, keepdims=True)


def list_other(early, stack2, late, slots, heads):
    side = early[SIDE]
    table = stack2[stack2.shape[0] - 16 :].astype(jnp.float32)[0:1]
    bits = jnp.zeros_like(table)
    for d in range(slots + 1):
        back = 2 * d + 1 - 2 * side
        match = (table == back.astype(jnp.float32)) & (back > 0)
        bits = bits + jnp.where(match, float(1 << d), 0.0)
    bits = jnp.sum(bits).astype(jnp.int32)
    late[0] = 0
    for d in range(slots + 1):
        @pl.when((early[OTHER + d] == 1) & (((bits >> d) & 1) == 1))
        def _(d=d):
            entry = late[0]
            late[1 + entry] = jnp.where(side == 0, d, slots - d)
            for h in range(heads):
                late[KEEP + heads * entry + h] = early[32 + heads * d + h]
            late[0] = entry + 1


def scores_kernel(early, stack, stack2, first_stats, same, exps, gprobs, key_t, stats, late):
    slots, rows, width = same.shape[0], same.shape[1], same.shape[2] // 2
    span = (stack.shape[0] - 16) // 2
    heads = span // rows
    scale = width ** (-0.5)
    f32 = jnp.float32

    list_other(early, stack2, late, slots, heads)
    stats[...] = jnp.zeros_like(stats)
    for which in range(2):
        stats[which, 0:1] = jnp.full((1, span), NEG, f32)
    stats[0, 3:6] = first_stats[0:3]

    for which, both, meta in ((0, stack, early), (1, stack2, late)):
        base = (slots - 1) * which

        def first(k, carry, which=which, both=both, base=base, meta=meta):
            i, slot = base + k, meta[1 + k]
            key_t[slot] = same[slot, :, :width].T
            for h in range(heads):
                part = slice(h * rows, (h + 1) * rows)
                s = lax.dot_general(
                    same[slot, :, :width], both[part], NT, preferred_element_type=f32
                )
                s = s * scale + jnp.where(meta[KEEP + heads * k + h] == 1, 0.0, NEG).astype(f32)
                exps[i, :, part] = s
                stats[which, 0:1, part] = jnp.maximum(
                    stats[which, 0:1, part], jnp.max(s, axis=0, keepdims=True)
                )
            return carry

        def second(k, carry, which=which, both=both, base=base, meta=meta):
            i, slot = base + k, meta[1 + k]
            for h in range(heads):
                part = slice(h * rows, (h + 1) * rows)
                g = lax.dot_general(
                    same[slot, :, width:], both[span + h * rows : span + (h + 1) * rows], NT, preferred_element_type=f32
                )
                e = jnp.exp(exps[i, :, part] - stats[which, 0:1, part])
                gprobs[i, :, part] = g
                exps[i, :, part] = e
                stats[which, 1:2, part] += jnp.sum(e, axis=0, keepdims=True)
                stats[which, 2:3, part] += jnp.sum(e * g, axis=0, keepdims=True)
            return carry

        lax.fori_loop(0, meta[0], first, 0)
        lax.fori_loop(0, meta[0], second, 0)


def terms_kernel(
    early, first, first_key_t, exps, gprobs, key_t, stack, stack2, mine, theirs,
    plane_ref, near_ref, dq_ref, factors, acc, probs, grads, late,
):
    rows, width = exps.shape[1], stack.shape[1]
    span = exps.shape[2]
    slots = plane_ref.shape[0]
    scale = width ** (-0.5)
    side = early[SIDE]
    stacks = (stack, stack2)
    list_other(early, stack2, late, slots, span // rows)
    f32, bf16 = jnp.float32, jnp.bfloat16

    def three(ref, which, row):
        return ref[which, row : row + 1], ref[which, row + 1 : row + 2], ref[which, row + 2 : row + 3]

    groups = (
        (three(mine, 0, 0), three(mine, 0, 3), three(theirs, 1, 0)),
        (three(mine, 1, 0), three(theirs, 0, 0), three(theirs, 0, 3)),
    )
    for which, group in enumerate(groups):
        high = functools.reduce(jnp.maximum, [top for top, _, _ in group])
        shares = [jnp.exp(top - high) for top, _, _ in group]
        total = sum(share * part for share, (_, part, _) in zip(shares, group))
        weighted = sum(share * part for share, (_, _, part) in zip(shares, group))
        inverse = 1.0 / total
        factors[which, 0:1] = shares[0] * inverse
        factors[which, 1:2] = weighted * inverse
        factors[which, 2:3] = shares[1] * inverse

    def gradients(load_e, load_g, keys, which, row):
        for h in range(span // rows):
            part = slice(h * rows, (h + 1) * rows)
            p = load_e(part) * factors[which, row : row + 1, part]
            probs[:, part] = p.astype(bf16)
            grads[:, part] = (p * (load_g(part) - factors[which, 1:2, part])).astype(bf16)
        key_term = jnp.dot(grads[...], stacks[which][:span], preferred_element_type=f32) * scale
        value_term = jnp.dot(probs[...], stacks[which][span : 2 * span], preferred_element_type=f32)
        return key_term, value_term, jnp.dot(keys, grads[...], preferred_element_type=f32)

    acc[...] = jnp.zeros_like(acc)
    key_term, value_term, dq_ref[0] = gradients(
        lambda part: first[0, :, part], lambda part: first[1, :, part], first_key_t[...], 0, 2
    )
    dq_ref[1] = jnp.zeros(dq_ref.shape[1:], f32)
    near_ref[:, :width] = key_term
    near_ref[:, width:] = value_term

    for which, meta in ((0, early), (1, late)):
        def step(k, carry, which=which, meta=meta):
            i, slot = (slots - 1) * which + k, meta[1 + k]
            key_term, value_term, query_term = gradients(
                lambda part: exps[i, :, part], lambda part: gprobs[i, :, part], key_t[slot], which, 0
            )
            dq_ref[which] += query_term
            acc[slot, :, :width] += key_term
            acc[slot, :, width:] += value_term
            return carry

        lax.fori_loop(0, meta[0], step, 0)
    for slot in range(1, slots):
        plane_ref[slot] = acc[slot].astype(bf16)

    @pl.when(side == 0)
    def _():
        near_ref[...] += acc[0]
        plane_ref[0] = jnp.zeros(plane_ref.shape[1:], bf16)

    @pl.when(side == 1)
    def _():
        plane_ref[0] = acc[0].astype(bf16)


def queries_kernel(mine, theirs, dq_ref):
    width, rows = mine.shape[1], dq_ref.shape[0]
    scale = width ** (-0.5)
    for h in range(dq_ref.shape[1] // width):
        part = slice(h * rows, (h + 1) * rows)
        dq = (mine[0, :, part] + theirs[:, part]) * scale
        dq_ref[:, h * width : (h + 1) * width] = dq.T.astype(dq_ref.dtype)


def plane_pairs(blocks, planes):
    pairs = []
    for block in range(blocks):
        for plane in range(planes):
            source = block - 2 * (plane if block % 2 == 0 else planes - plane)
            if source >= 0:
                pairs.append((source * planes + plane, block * planes + plane))
    return pairs


def local(queries, keys, values, grad_out, doc_of_block, pair_list, knock):
    rows, width = keys.shape
    heads = queries.shape[1] // width
    reach = pair_list.shape[1] + 1
    blocks = doc_of_block.shape[0]
    planes = lax.axis_size("head")
    here = lax.axis_index("ctx")
    info = jnp.stack([here, here % 2])
    out = plane_pairs(blocks, planes)
    back = [(b, a) for a, b in out if a != b]
    swap = [(i, i ^ 1) for i in range(blocks)]
    bf16, f32 = jnp.bfloat16, jnp.float32
    span = heads * rows

    edge = jnp.zeros((), bf16)
    own = lax.pad(keys, edge, ((0, 0, 0), (0, width, 0))) + lax.pad(values, edge, ((0, 0, 0), (width, 0, 0)))
    fetched = lax.ppermute(own, BOTH, out)
    vmem = pl.BlockSpec(memory_space=pltpu.VMEM)
    smem = pl.BlockSpec(memory_space=pltpu.SMEM)

    def grant(mebibytes):
        return pltpu.CompilerParams(vmem_limit_bytes=mebibytes << 20)

    work = pl.CostEstimate(flops=10**10, bytes_accessed=1 << 22, transcendentals=0)
    lists = jax.ShapeDtypeStruct((32 + heads * (planes + 1),), jnp.int32)
    early = pl.pallas_call(
        list_kernel,
        out_shape=lists,
        in_specs=[smem] * 4,
        out_specs=smem,
        compiler_params=grant(GRANT),
        cost_estimate=work,
    )(info, doc_of_block, pair_list, knock)
    far = pl.BlockSpec(memory_space=pltpu.HBM)
    both0, key0_t, stack, stats0 = pl.pallas_call(
        first_kernel,
        out_shape=(
            pltpu.VMEM((2, rows, span), f32),
            pltpu.VMEM((width, rows), bf16),
            jax.ShapeDtypeStruct((2 * span + 16, width), bf16),
            jax.ShapeDtypeStruct((8, span), f32),
        ),
        in_specs=[far, far, vmem, vmem],
        out_specs=(vmem,) * 4,
        scratch_shapes=[pltpu.SemaphoreType.DMA((2 * heads,))],
        compiler_params=grant(GRANT),
        cost_estimate=work,
    )(*(pltpu.with_memory_space_constraint(x, pltpu.HBM) for x in (queries, grad_out)), own, pair_list)
    stack2 = lax.ppermute(stack, "ctx", swap)
    fetched, stats0, early = lax.optimization_barrier((fetched, stats0, early))
    same = lax.all_to_all(jnp.broadcast_to(fetched, (planes, rows, 2 * width)), "head", 0, 0)
    exps, gprobs, key_t, mine = pl.pallas_call(
        scores_kernel,
        out_shape=(
            pltpu.VMEM((reach - 1, rows, span), f32),
            pltpu.VMEM((reach - 1, rows, span), f32),
            pltpu.VMEM((planes, width, rows), bf16),
            jax.ShapeDtypeStruct((2, 8, span), f32),
        ),
        in_specs=[smem] + [vmem] * 4,
        out_specs=(vmem,) * 4,
        scratch_shapes=[pltpu.SMEM((32,), jnp.int32)],
        compiler_params=grant(GRANT),
    )(early, stack, stack2, stats0, same)
    theirs = lax.ppermute(mine, "ctx", swap)
    plane, near, dq = pl.pallas_call(
        terms_kernel,
        out_shape=(
            jax.ShapeDtypeStruct((planes, rows, 2 * width), bf16),
            jax.ShapeDtypeStruct((rows, 2 * width), f32),
            jax.ShapeDtypeStruct((2, width, span), f32),
        ),
        in_specs=[smem] + [vmem] * 9,
        out_specs=(vmem,) * 3,
        scratch_shapes=[
            pltpu.VMEM((2, 8, span), f32),
            pltpu.VMEM((planes, rows, 2 * width), f32),
            pltpu.VMEM((rows, span), bf16),
            pltpu.VMEM((rows, span), bf16),
            pltpu.SMEM((32,), jnp.int32),
        ],
        compiler_params=grant(GRANT),
    )(early, both0, key0_t, exps, gprobs, key_t, stack, stack2, mine, theirs)

    parts = lax.all_to_all(plane, "head", 0, 0)
    sent = jnp.sum(parts.astype(f32), axis=0).astype(bf16)
    landed = lax.ppermute(sent, BOTH, back)
    dq2 = lax.ppermute(dq[1], "ctx", swap)
    d_queries = pl.pallas_call(
        queries_kernel,
        out_shape=jax.ShapeDtypeStruct(queries.shape, bf16),
        in_specs=[vmem] * 2,
        out_specs=vmem,
    )(dq, dq2)
    mine = (landed.astype(f32) + near).astype(bf16)
    every = lax.all_to_all(jnp.broadcast_to(mine, (planes, rows, 2 * width)), "head", 0, 0)
    d_keys = sum(every[i, :, :width].astype(f32) for i in range(planes)).astype(bf16)
    d_values = sum(every[i, :, width:].astype(f32) for i in range(planes)).astype(bf16)
    return d_queries, d_keys, d_values


def solution(mesh):
    in_specs = (
        P("ctx", "head"),
        P("ctx", None),
        P("ctx", None),
        P("ctx", "head"),
        P(),
        P("ctx", None),
        P("head", None),
    )
    out_specs = (P("ctx", "head"), P("ctx", None), P("ctx", None))
    return jax.shard_map(local, mesh=mesh, in_specs=in_specs, out_specs=out_specs, check_vma=False)
```

```python
import functools

import jax
import jax.numpy as jnp
from jax import lax
from jax.experimental import pallas as pl
from jax.experimental.pallas import tpu as pltpu
from jax.sharding import PartitionSpec as P

NEG = -1e30
BOTH = ("ctx", "head")
NT = (((1,), (1,)), ((), ()))
GRANT = 12


KEEP, OTHER, SIDE = 8, 24, 30


def list_kernel(info, docs, pairs, knock, early):
    heads, slots = knock.shape[0], (pairs.shape[1] + 1) // 2
    here, side = info[0], info[1]
    early[0] = 0
    early[SIDE] = side
    for d in range(slots + 1):
        block = jnp.maximum(here - 2 * d, 0)
        kept = functools.reduce(jnp.logical_or, [knock[h, block] == 1 for h in range(heads)])
        kept = kept & (here - 2 * d >= 0)
        back = 2 * d + 1 - 2 * side
        query = here + 1 - 2 * side
        candidate = (back > 0) & (back < 2 * slots) & kept & (docs[block] == docs[query])
        early[OTHER + d] = jnp.where(candidate, 1, 0)
        for h in range(heads):
            early[32 + heads * d + h] = knock[h, block]
        if 0 < d < slots:
            listed = functools.reduce(
                jnp.logical_or, [pairs[0, k] == 2 * d for k in range(pairs.shape[1])]
            )

            @pl.when(kept & listed & (docs[block] == docs[here]))
            def _(d=d, block=block):
                entry = early[0]
                early[1 + entry] = jnp.where(side == 0, d, slots - d)
                for h in range(heads):
                    early[KEEP + heads * entry + h] = knock[h, block]
                early[0] = entry + 1


def first_kernel(q_ref, g_ref, own, pairs, both, key_t, stack, stats, arrivals):
    rows, width = own.shape[0], own.shape[1] // 2
    heads = q_ref.shape[1] // width
    span = heads * rows
    scale = width ** (-0.5)
    f32 = jnp.float32

    copies = []
    for n, source in enumerate((q_ref, g_ref)):
        for h in range(heads):
            place = n * span + h * rows
            copy = pltpu.make_async_copy(
                source.at[:, pl.ds(h * width, width)],
                stack.at[pl.ds(place, rows)],
                arrivals.at[n * heads + h],
            )
            copy.start()
            copies.append(copy)
    stack[2 * span :] = jnp.zeros((16, width), stack.dtype)
    listed = jnp.broadcast_to(pairs[...].astype(f32), (16, pairs.shape[1]))
    stack[2 * span :, : pairs.shape[1]] = listed.astype(stack.dtype)
    key_t[...] = own[:, :width].T
    stats[...] = jnp.zeros_like(stats)
    below = lax.broadcasted_iota(jnp.int32, (rows, rows), 0) <= lax.broadcasted_iota(
        jnp.int32, (rows, rows), 1
    )
    for copy in copies:
        copy.wait()
    for h in range(heads):
        part = slice(h * rows, (h + 1) * rows)
        late_part = slice(span + h * rows, span + (h + 1) * rows)
        s = lax.dot_general(own[:, :width], stack[part], NT, preferred_element_type=f32) * scale
        g = lax.dot_general(own[:, width:], stack[late_part], NT, preferred_element_type=f32)
        s = jnp.where(below, s, NEG)
        top = jnp.max(s, axis=0, keepdims=True)
        e = jnp.exp(s - top)
        both[0, :, part] = e
        both[1, :, part] = g
        stats[0:1, part] = top
        stats[1:2, part] = jnp.sum(e, axis=0, keepdims=True)
        stats[2:3, part] = jnp.sum(e * g, axis=0, keepdims=True)


def list_other(early, stack2, late, slots, heads):
    side = early[SIDE]
    table = stack2[stack2.shape[0] - 16 :].astype(jnp.float32)[0:1]
    bits = jnp.zeros_like(table)
    for d in range(slots + 1):
        back = 2 * d + 1 - 2 * side
        match = (table == back.astype(jnp.float32)) & (back > 0)
        bits = bits + jnp.where(match, float(1 << d), 0.0)
    bits = jnp.sum(bits).astype(jnp.int32)
    late[0] = 0
    for d in range(slots + 1):
        @pl.when((early[OTHER + d] == 1) & (((bits >> d) & 1) == 1))
        def _(d=d):
            entry = late[0]
            late[1 + entry] = jnp.where(side == 0, d, slots - d)
            for h in range(heads):
                late[KEEP + heads * entry + h] = early[32 + heads * d + h]
            late[0] = entry + 1


def scores_kernel(early, stack, stack2, first_stats, same, exps, gprobs, key_t, tops, stats, late):
    slots, rows, width = same.shape[0], same.shape[1], same.shape[2] // 2
    span = (stack.shape[0] - 16) // 2
    heads = span // rows
    scale = width ** (-0.5)
    f32 = jnp.float32

    list_other(early, stack2, late, slots, heads)
    stats[...] = jnp.zeros_like(stats)
    for which in range(2):
        stats[which, 0:1] = jnp.full((1, span), NEG, f32)
    stats[0, 3:6] = first_stats[0:3]

    for which, both, meta in ((0, stack, early), (1, stack2, late)):
        base = (slots - 1) * which

        def tile(k, carry, which=which, both=both, base=base, meta=meta):
            i, slot = base + k, meta[1 + k]
            key_t[slot] = same[slot, :, :width].T
            for h in range(heads):
                part = slice(h * rows, (h + 1) * rows)
                s = lax.dot_general(
                    same[slot, :, :width], both[part], NT, preferred_element_type=f32
                )
                g = lax.dot_general(
                    same[slot, :, width:],
                    both[span + h * rows : span + (h + 1) * rows],
                    NT,
                    preferred_element_type=f32,
                )
                s = s * scale + jnp.where(meta[KEEP + heads * k + h] == 1, 0.0, NEG).astype(f32)
                top = jnp.max(s, axis=0, keepdims=True)
                e = jnp.exp(s - top)
                exps[i, :, part] = e
                gprobs[i, :, part] = g
                tops[i, 0:1, part] = top
                before = stats[which, 0:1, part]
                high = jnp.maximum(before, top)
                old, new = jnp.exp(before - high), jnp.exp(top - high)
                total = jnp.sum(e, axis=0, keepdims=True)
                weighted = jnp.sum(e * g, axis=0, keepdims=True)
                stats[which, 0:1, part] = high
                stats[which, 1:2, part] = stats[which, 1:2, part] * old + total * new
                stats[which, 2:3, part] = stats[which, 2:3, part] * old + weighted * new
            return carry

        lax.fori_loop(0, meta[0], tile, 0)


def terms_kernel(
    early, first, first_key_t, exps, gprobs, key_t, tops, stack, stack2, mine, theirs,
    plane_ref, near_ref, dq_ref, factors, acc, probs, grads, late,
):
    rows, width = exps.shape[1], stack.shape[1]
    span = exps.shape[2]
    slots = plane_ref.shape[0]
    scale = width ** (-0.5)
    side = early[SIDE]
    stacks = (stack, stack2)
    list_other(early, stack2, late, slots, span // rows)
    f32, bf16 = jnp.float32, jnp.bfloat16

    def three(ref, which, row):
        return ref[which, row : row + 1], ref[which, row + 1 : row + 2], ref[which, row + 2 : row + 3]

    groups = (
        (three(mine, 0, 0), three(mine, 0, 3), three(theirs, 1, 0)),
        (three(mine, 1, 0), three(theirs, 0, 0), three(theirs, 0, 3)),
    )
    for which, group in enumerate(groups):
        high = functools.reduce(jnp.maximum, [top for top, _, _ in group])
        shares = [jnp.exp(top - high) for top, _, _ in group]
        total = sum(share * part for share, (_, part, _) in zip(shares, group))
        weighted = sum(share * part for share, (_, _, part) in zip(shares, group))
        inverse = 1.0 / total
        factors[which, 0:1] = high
        factors[which, 1:2] = weighted * inverse
        factors[which, 2:3] = shares[1] * inverse
        factors[which, 3:4] = inverse

    def gradients(load_e, load_g, keys, which, factor):
        for h in range(span // rows):
            part = slice(h * rows, (h + 1) * rows)
            p = load_e(part) * factor(part)
            probs[:, part] = p.astype(bf16)
            grads[:, part] = (p * (load_g(part) - factors[which, 1:2, part])).astype(bf16)
        key_term = jnp.dot(grads[...], stacks[which][:span], preferred_element_type=f32) * scale
        value_term = jnp.dot(probs[...], stacks[which][span : 2 * span], preferred_element_type=f32)
        return key_term, value_term, jnp.dot(keys, grads[...], preferred_element_type=f32)

    acc[...] = jnp.zeros_like(acc)
    key_term, value_term, dq_ref[0] = gradients(
        lambda part: first[0, :, part], lambda part: first[1, :, part], first_key_t[...], 0,
        lambda part: factors[0, 2:3, part],
    )
    dq_ref[1] = jnp.zeros(dq_ref.shape[1:], f32)
    near_ref[:, :width] = key_term
    near_ref[:, width:] = value_term

    for which, meta in ((0, early), (1, late)):
        def step(k, carry, which=which, meta=meta):
            i, slot = (slots - 1) * which + k, meta[1 + k]
            key_term, value_term, query_term = gradients(
                lambda part: exps[i, :, part], lambda part: gprobs[i, :, part], key_t[slot], which,
                lambda part: jnp.exp(tops[i, 0:1, part] - factors[which, 0:1, part])
                * factors[which, 3:4, part],
            )
            dq_ref[which] += query_term
            acc[slot, :, :width] += key_term
            acc[slot, :, width:] += value_term
            return carry

        lax.fori_loop(0, meta[0], step, 0)
    for slot in range(1, slots):
        plane_ref[slot] = acc[slot].astype(bf16)

    @pl.when(side == 0)
    def _():
        near_ref[...] += acc[0]
        plane_ref[0] = jnp.zeros(plane_ref.shape[1:], bf16)

    @pl.when(side == 1)
    def _():
        plane_ref[0] = acc[0].astype(bf16)


def queries_kernel(mine, theirs, dq_ref):
    width, rows = mine.shape[1], dq_ref.shape[0]
    scale = width ** (-0.5)
    for h in range(dq_ref.shape[1] // width):
        part = slice(h * rows, (h + 1) * rows)
        dq = (mine[0, :, part] + theirs[:, part]) * scale
        dq_ref[:, h * width : (h + 1) * width] = dq.T.astype(dq_ref.dtype)


def plane_pairs(blocks, planes):
    pairs = []
    for block in range(blocks):
        for plane in range(planes):
            source = block - 2 * (plane if block % 2 == 0 else planes - plane)
            if source >= 0:
                pairs.append((source * planes + plane, block * planes + plane))
    return pairs


def local(queries, keys, values, grad_out, doc_of_block, pair_list, knock):
    rows, width = keys.shape
    heads = queries.shape[1] // width
    reach = pair_list.shape[1] + 1
    blocks = doc_of_block.shape[0]
    planes = lax.axis_size("head")
    here = lax.axis_index("ctx")
    info = jnp.stack([here, here % 2])
    out = plane_pairs(blocks, planes)
    back = [(b, a) for a, b in out if a != b]
    swap = [(i, i ^ 1) for i in range(blocks)]
    bf16, f32 = jnp.bfloat16, jnp.float32
    span = heads * rows

    edge = jnp.zeros((), bf16)
    own = lax.pad(keys, edge, ((0, 0, 0), (0, width, 0))) + lax.pad(values, edge, ((0, 0, 0), (width, 0, 0)))
    fetched = lax.ppermute(own, BOTH, out)
    vmem = pl.BlockSpec(memory_space=pltpu.VMEM)
    smem = pl.BlockSpec(memory_space=pltpu.SMEM)

    def grant(mebibytes):
        return pltpu.CompilerParams(vmem_limit_bytes=mebibytes << 20)

    work = pl.CostEstimate(flops=10**10, bytes_accessed=1 << 22, transcendentals=0)
    lists = jax.ShapeDtypeStruct((32 + heads * (planes + 1),), jnp.int32)
    early = pl.pallas_call(
        list_kernel,
        out_shape=lists,
        in_specs=[smem] * 4,
        out_specs=smem,
        compiler_params=grant(GRANT),
        cost_estimate=work,
    )(info, doc_of_block, pair_list, knock)
    far = pl.BlockSpec(memory_space=pltpu.HBM)
    both0, key0_t, stack, stats0 = pl.pallas_call(
        first_kernel,
        out_shape=(
            pltpu.VMEM((2, rows, span), f32),
            pltpu.VMEM((width, rows), bf16),
            jax.ShapeDtypeStruct((2 * span + 16, width), bf16),
            jax.ShapeDtypeStruct((8, span), f32),
        ),
        in_specs=[far, far, vmem, vmem],
        out_specs=(vmem,) * 4,
        scratch_shapes=[pltpu.SemaphoreType.DMA((2 * heads,))],
        compiler_params=grant(GRANT),
        cost_estimate=work,
    )(*(pltpu.with_memory_space_constraint(x, pltpu.HBM) for x in (queries, grad_out)), own, pair_list)
    stack2 = lax.ppermute(stack, "ctx", swap)
    fetched, stats0, early = lax.optimization_barrier((fetched, stats0, early))
    same = lax.all_to_all(jnp.broadcast_to(fetched, (planes, rows, 2 * width)), "head", 0, 0)
    exps, gprobs, key_t, tops, mine = pl.pallas_call(
        scores_kernel,
        out_shape=(
            pltpu.VMEM((reach - 1, rows, span), f32),
            pltpu.VMEM((reach - 1, rows, span), f32),
            pltpu.VMEM((planes, width, rows), bf16),
            pltpu.VMEM((reach - 1, 8, span), f32),
            jax.ShapeDtypeStruct((2, 8, span), f32),
        ),
        in_specs=[smem] + [vmem] * 4,
        out_specs=(vmem,) * 5,
        scratch_shapes=[pltpu.SMEM((32,), jnp.int32)],
        compiler_params=grant(GRANT),
    )(early, stack, stack2, stats0, same)
    theirs = lax.ppermute(mine, "ctx", swap)
    plane, near, dq = pl.pallas_call(
        terms_kernel,
        out_shape=(
            jax.ShapeDtypeStruct((planes, rows, 2 * width), bf16),
            jax.ShapeDtypeStruct((rows, 2 * width), f32),
            jax.ShapeDtypeStruct((2, width, span), f32),
        ),
        in_specs=[smem] + [vmem] * 10,
        out_specs=(vmem,) * 3,
        scratch_shapes=[
            pltpu.VMEM((2, 8, span), f32),
            pltpu.VMEM((planes, rows, 2 * width), f32),
            pltpu.VMEM((rows, span), bf16),
            pltpu.VMEM((rows, span), bf16),
            pltpu.SMEM((32,), jnp.int32),
        ],
        compiler_params=grant(GRANT),
    )(early, both0, key0_t, exps, gprobs, key_t, tops, stack, stack2, mine, theirs)

    parts = lax.all_to_all(plane, "head", 0, 0)
    sent = jnp.sum(parts.astype(f32), axis=0).astype(bf16)
    landed = lax.ppermute(sent, BOTH, back)
    dq2 = lax.ppermute(dq[1], "ctx", swap)
    d_queries = pl.pallas_call(
        queries_kernel,
        out_shape=jax.ShapeDtypeStruct(queries.shape, bf16),
        in_specs=[vmem] * 2,
        out_specs=vmem,
    )(dq, dq2)
    mine = (landed.astype(f32) + near).astype(bf16)
    every = lax.all_to_all(jnp.broadcast_to(mine, (planes, rows, 2 * width)), "head", 0, 0)
    d_keys = sum(every[i, :, :width].astype(f32) for i in range(planes)).astype(bf16)
    d_values = sum(every[i, :, width:].astype(f32) for i in range(planes)).astype(bf16)
    return d_queries, d_keys, d_values


def solution(mesh):
    in_specs = (
        P("ctx", "head"),
        P("ctx", None),
        P("ctx", None),
        P("ctx", "head"),
        P(),
        P("ctx", None),
        P("head", None),
    )
    out_specs = (P("ctx", "head"), P("ctx", None), P("ctx", None))
    return jax.shard_map(local, mesh=mesh, in_specs=in_specs, out_specs=out_specs, check_vma=False)
```

```python
import functools

import jax
import jax.numpy as jnp
from jax import lax
from jax.experimental import pallas as pl
from jax.experimental.pallas import tpu as pltpu
from jax.sharding import PartitionSpec as P

NEG = -1e30
BOTH = ("ctx", "head")
NT = (((1,), (1,)), ((), ()))
GRANT = 12


KEEP, OTHER, SIDE = 8, 24, 30


def list_kernel(info, docs, pairs, knock, early):
    heads, slots = knock.shape[0], (pairs.shape[1] + 1) // 2
    here, side = info[0], info[1]
    early[0] = 0
    early[SIDE] = side
    for d in range(slots + 1):
        block = jnp.maximum(here - 2 * d, 0)
        kept = functools.reduce(jnp.logical_or, [knock[h, block] == 1 for h in range(heads)])
        kept = kept & (here - 2 * d >= 0)
        back = 2 * d + 1 - 2 * side
        query = here + 1 - 2 * side
        candidate = (back > 0) & (back < 2 * slots) & kept & (docs[block] == docs[query])
        early[OTHER + d] = jnp.where(candidate, 1, 0)
        for h in range(heads):
            early[32 + heads * d + h] = knock[h, block]
        if 0 < d < slots:
            listed = functools.reduce(
                jnp.logical_or, [pairs[0, k] == 2 * d for k in range(pairs.shape[1])]
            )

            @pl.when(kept & listed & (docs[block] == docs[here]))
            def _(d=d, block=block):
                entry = early[0]
                early[1 + entry] = jnp.where(side == 0, d, slots - d)
                for h in range(heads):
                    early[KEEP + heads * entry + h] = knock[h, block]
                early[0] = entry + 1


def first_kernel(q_ref, g_ref, own, pairs, exps, gprobs, key_t, stack, stats, arrivals):
    rows, width = own.shape[0], own.shape[1] // 2
    heads = q_ref.shape[1] // width
    span = heads * rows
    scale = width ** (-0.5)
    f32 = jnp.float32

    copies = []
    for n, source in enumerate((q_ref, g_ref)):
        for h in range(heads):
            place = n * span + h * rows
            copy = pltpu.make_async_copy(
                source.at[:, pl.ds(h * width, width)],
                stack.at[pl.ds(place, rows)],
                arrivals.at[n * heads + h],
            )
            copy.start()
            copies.append(copy)
    stack[2 * span :] = jnp.zeros((16, width), stack.dtype)
    listed = jnp.broadcast_to(pairs[...].astype(f32), (16, pairs.shape[1]))
    stack[2 * span :, : pairs.shape[1]] = listed.astype(stack.dtype)
    key_t[...] = own[:, :width].T
    stats[...] = jnp.zeros_like(stats)
    below = lax.broadcasted_iota(jnp.int32, (rows, rows), 0) <= lax.broadcasted_iota(
        jnp.int32, (rows, rows), 1
    )
    for copy in copies:
        copy.wait()
    for h in range(heads):
        part = slice(h * rows, (h + 1) * rows)
        late_part = slice(span + h * rows, span + (h + 1) * rows)
        s = lax.dot_general(own[:, :width], stack[part], NT, preferred_element_type=f32) * scale
        g = lax.dot_general(own[:, width:], stack[late_part], NT, preferred_element_type=f32)
        s = jnp.where(below, s, NEG)
        top = jnp.max(s, axis=0, keepdims=True)
        e = jnp.exp(s - top)
        exps[:, part] = e
        gprobs[:, part] = g
        stats[0:1, part] = top
        stats[1:2, part] = jnp.sum(e, axis=0, keepdims=True)
        stats[2:3, part] = jnp.sum(e * g, axis=0, keepdims=True)


def list_other(early, stack2, late, slots, heads):
    side = early[SIDE]
    table = stack2[stack2.shape[0] - 16 :].astype(jnp.float32)[0:1]
    bits = jnp.zeros_like(table)
    for d in range(slots + 1):
        back = 2 * d + 1 - 2 * side
        match = (table == back.astype(jnp.float32)) & (back > 0)
        bits = bits + jnp.where(match, float(1 << d), 0.0)
    bits = jnp.sum(bits).astype(jnp.int32)
    late[0] = 0
    for d in range(slots + 1):
        @pl.when((early[OTHER + d] == 1) & (((bits >> d) & 1) == 1))
        def _(d=d):
            entry = late[0]
            late[1 + entry] = jnp.where(side == 0, d, slots - d)
            for h in range(heads):
                late[KEEP + heads * entry + h] = early[32 + heads * d + h]
            late[0] = entry + 1


def scores_kernel(early, stack, stack2, first_stats, same, exps, gprobs, key_t, tops, stats, late):
    slots, rows, width = same.shape[0], same.shape[1], same.shape[2] // 2
    span = (stack.shape[0] - 16) // 2
    heads = span // rows
    scale = width ** (-0.5)
    f32 = jnp.float32

    list_other(early, stack2, late, slots, heads)
    stats[...] = jnp.zeros_like(stats)
    for which in range(2):
        stats[which, 0:1] = jnp.full((1, span), NEG, f32)
    stats[0, 3:6] = first_stats[0:3]

    for which, both, meta in ((0, stack, early), (1, stack2, late)):
        base = (slots - 1) * which

        def tile(k, carry, which=which, both=both, base=base, meta=meta):
            i, slot = base + k, meta[1 + k]
            key_t[slot] = same[slot, :, :width].T
            for h in range(heads):
                part = slice(h * rows, (h + 1) * rows)
                s = lax.dot_general(
                    same[slot, :, :width], both[part], NT, preferred_element_type=f32
                )
                g = lax.dot_general(
                    same[slot, :, width:],
                    both[span + h * rows : span + (h + 1) * rows],
                    NT,
                    preferred_element_type=f32,
                )
                s = s * scale + jnp.where(meta[KEEP + heads * k + h] == 1, 0.0, NEG).astype(f32)
                top = jnp.max(s, axis=0, keepdims=True)
                e = jnp.exp(s - top)
                exps[i, :, part] = e
                gprobs[i, :, part] = g
                tops[i, 0:1, part] = top
                before = stats[which, 0:1, part]
                high = jnp.maximum(before, top)
                old, new = jnp.exp(before - high), jnp.exp(top - high)
                total = jnp.sum(e, axis=0, keepdims=True)
                weighted = jnp.sum(e * g, axis=0, keepdims=True)
                stats[which, 0:1, part] = high
                stats[which, 1:2, part] = stats[which, 1:2, part] * old + total * new
                stats[which, 2:3, part] = stats[which, 2:3, part] * old + weighted * new
            return carry

        lax.fori_loop(0, meta[0], tile, 0)


def terms_kernel(
    early, first_exps, first_gprobs, first_key_t, exps, gprobs, key_t, tops, stack, stack2, mine, theirs,
    plane_ref, near_ref, dq_ref, factors, acc, probs, grads, late,
):
    rows, width = exps.shape[1], stack.shape[1]
    span = exps.shape[2]
    slots = plane_ref.shape[0]
    scale = width ** (-0.5)
    side = early[SIDE]
    stacks = (stack, stack2)
    list_other(early, stack2, late, slots, span // rows)
    f32, bf16 = jnp.float32, jnp.bfloat16

    def three(ref, which, row):
        return ref[which, row : row + 1], ref[which, row + 1 : row + 2], ref[which, row + 2 : row + 3]

    groups = (
        (three(mine, 0, 0), three(mine, 0, 3), three(theirs, 1, 0)),
        (three(mine, 1, 0), three(theirs, 0, 0), three(theirs, 0, 3)),
    )
    for which, group in enumerate(groups):
        high = functools.reduce(jnp.maximum, [top for top, _, _ in group])
        shares = [jnp.exp(top - high) for top, _, _ in group]
        total = sum(share * part for share, (_, part, _) in zip(shares, group))
        weighted = sum(share * part for share, (_, _, part) in zip(shares, group))
        inverse = 1.0 / total
        factors[which, 0:1] = high
        factors[which, 1:2] = weighted * inverse
        factors[which, 2:3] = shares[1] * inverse
        factors[which, 3:4] = inverse

    def gradients(load_e, load_g, keys, which, factor):
        for h in range(span // rows):
            part = slice(h * rows, (h + 1) * rows)
            p = load_e(part) * factor(part)
            probs[:, part] = p.astype(bf16)
            grads[:, part] = (p * (load_g(part) - factors[which, 1:2, part])).astype(bf16)
        key_term = jnp.dot(grads[...], stacks[which][:span], preferred_element_type=f32) * scale
        value_term = jnp.dot(probs[...], stacks[which][span : 2 * span], preferred_element_type=f32)
        return key_term, value_term, jnp.dot(keys, grads[...], preferred_element_type=f32)

    acc[...] = jnp.zeros_like(acc)
    key_term, value_term, dq_ref[0] = gradients(
        lambda part: first_exps[:, part], lambda part: first_gprobs[:, part], first_key_t[...], 0,
        lambda part: factors[0, 2:3, part],
    )
    dq_ref[1] = jnp.zeros(dq_ref.shape[1:], f32)
    near_ref[:, :width] = key_term
    near_ref[:, width:] = value_term

    for which, meta in ((0, early), (1, late)):
        def step(k, carry, which=which, meta=meta):
            i, slot = (slots - 1) * which + k, meta[1 + k]
            key_term, value_term, query_term = gradients(
                lambda part: exps[i, :, part], lambda part: gprobs[i, :, part], key_t[slot], which,
                lambda part: jnp.exp(tops[i, 0:1, part] - factors[which, 0:1, part])
                * factors[which, 3:4, part],
            )
            dq_ref[which] += query_term
            acc[slot, :, :width] += key_term
            acc[slot, :, width:] += value_term
            return carry

        lax.fori_loop(0, meta[0], step, 0)
    for slot in range(1, slots):
        plane_ref[slot] = acc[slot].astype(bf16)

    @pl.when(side == 0)
    def _():
        near_ref[...] += acc[0]
        plane_ref[0] = jnp.zeros(plane_ref.shape[1:], bf16)

    @pl.when(side == 1)
    def _():
        plane_ref[0] = acc[0].astype(bf16)


def queries_kernel(mine, theirs, dq_ref):
    width, rows = mine.shape[1], dq_ref.shape[0]
    scale = width ** (-0.5)
    for h in range(dq_ref.shape[1] // width):
        part = slice(h * rows, (h + 1) * rows)
        dq = (mine[0, :, part] + theirs[:, part]) * scale
        dq_ref[:, h * width : (h + 1) * width] = dq.T.astype(dq_ref.dtype)


def plane_pairs(blocks, planes):
    pairs = []
    for block in range(blocks):
        for plane in range(planes):
            source = block - 2 * (plane if block % 2 == 0 else planes - plane)
            if source >= 0:
                pairs.append((source * planes + plane, block * planes + plane))
    return pairs


def local(queries, keys, values, grad_out, doc_of_block, pair_list, knock):
    rows, width = keys.shape
    heads = queries.shape[1] // width
    reach = pair_list.shape[1] + 1
    blocks = doc_of_block.shape[0]
    planes = lax.axis_size("head")
    here = lax.axis_index("ctx")
    info = jnp.stack([here, here % 2])
    out = plane_pairs(blocks, planes)
    back = [(b, a) for a, b in out if a != b]
    swap = [(i, i ^ 1) for i in range(blocks)]
    bf16, f32 = jnp.bfloat16, jnp.float32
    span = heads * rows

    edge = jnp.zeros((), bf16)
    own = lax.pad(keys, edge, ((0, 0, 0), (0, width, 0))) + lax.pad(values, edge, ((0, 0, 0), (width, 0, 0)))
    fetched = lax.ppermute(own, BOTH, out)
    vmem = pl.BlockSpec(memory_space=pltpu.VMEM)
    smem = pl.BlockSpec(memory_space=pltpu.SMEM)

    def grant(mebibytes):
        return pltpu.CompilerParams(vmem_limit_bytes=mebibytes << 20)

    work = pl.CostEstimate(flops=10**10, bytes_accessed=1 << 22, transcendentals=0)
    lists = jax.ShapeDtypeStruct((32 + heads * (planes + 1),), jnp.int32)
    early = pl.pallas_call(
        list_kernel,
        out_shape=lists,
        in_specs=[smem] * 4,
        out_specs=smem,
        compiler_params=grant(GRANT),
        cost_estimate=work,
    )(info, doc_of_block, pair_list, knock)
    far = pl.BlockSpec(memory_space=pltpu.HBM)
    exps0, gprobs0, key0_t, stack, stats0 = pl.pallas_call(
        first_kernel,
        out_shape=(
            pltpu.VMEM((rows, span), f32),
            pltpu.VMEM((rows, span), f32),
            pltpu.VMEM((width, rows), bf16),
            jax.ShapeDtypeStruct((2 * span + 16, width), bf16),
            jax.ShapeDtypeStruct((8, span), f32),
        ),
        in_specs=[far, far, vmem, vmem],
        out_specs=(vmem,) * 5,
        scratch_shapes=[pltpu.SemaphoreType.DMA((2 * heads,))],
        compiler_params=grant(GRANT),
        cost_estimate=work,
    )(*(pltpu.with_memory_space_constraint(x, pltpu.HBM) for x in (queries, grad_out)), own, pair_list)
    stack2 = lax.ppermute(stack, "ctx", swap)
    fetched, stats0, early = lax.optimization_barrier((fetched, stats0, early))
    same = lax.all_to_all(jnp.broadcast_to(fetched, (planes, rows, 2 * width)), "head", 0, 0)
    exps, gprobs, key_t, tops, mine = pl.pallas_call(
        scores_kernel,
        out_shape=(
            pltpu.VMEM((reach - 1, rows, span), f32),
            pltpu.VMEM((reach - 1, rows, span), f32),
            pltpu.VMEM((planes, width, rows), bf16),
            pltpu.VMEM((reach - 1, 8, span), f32),
            jax.ShapeDtypeStruct((2, 8, span), f32),
        ),
        in_specs=[smem] + [vmem] * 4,
        out_specs=(vmem,) * 5,
        scratch_shapes=[pltpu.SMEM((32,), jnp.int32)],
        compiler_params=grant(GRANT),
    )(early, stack, stack2, stats0, same)
    theirs = lax.ppermute(mine, "ctx", swap)
    plane, near, dq = pl.pallas_call(
        terms_kernel,
        out_shape=(
            jax.ShapeDtypeStruct((planes, rows, 2 * width), bf16),
            jax.ShapeDtypeStruct((rows, 2 * width), f32),
            jax.ShapeDtypeStruct((2, width, span), f32),
        ),
        in_specs=[smem] + [vmem] * 11,
        out_specs=(vmem,) * 3,
        scratch_shapes=[
            pltpu.VMEM((2, 8, span), f32),
            pltpu.VMEM((planes, rows, 2 * width), f32),
            pltpu.VMEM((rows, span), bf16),
            pltpu.VMEM((rows, span), bf16),
            pltpu.SMEM((32,), jnp.int32),
        ],
        compiler_params=grant(GRANT),
    )(early, exps0, gprobs0, key0_t, exps, gprobs, key_t, tops, stack, stack2, mine, theirs)

    parts = lax.all_to_all(plane, "head", 0, 0)
    sent = jnp.sum(parts.astype(f32), axis=0).astype(bf16)
    landed = lax.ppermute(sent, BOTH, back)
    dq2 = lax.ppermute(dq[1], "ctx", swap)
    d_queries = pl.pallas_call(
        queries_kernel,
        out_shape=jax.ShapeDtypeStruct(queries.shape, bf16),
        in_specs=[vmem] * 2,
        out_specs=vmem,
    )(dq, dq2)
    mine = (landed.astype(f32) + near).astype(bf16)
    every = lax.all_to_all(jnp.broadcast_to(mine, (planes, rows, 2 * width)), "head", 0, 0)
    d_keys = sum(every[i, :, :width].astype(f32) for i in range(planes)).astype(bf16)
    d_values = sum(every[i, :, width:].astype(f32) for i in range(planes)).astype(bf16)
    return d_queries, d_keys, d_values


def solution(mesh):
    in_specs = (
        P("ctx", "head"),
        P("ctx", None),
        P("ctx", None),
        P("ctx", "head"),
        P(),
        P("ctx", None),
        P("head", None),
    )
    out_specs = (P("ctx", "head"), P("ctx", None), P("ctx", None))
    return jax.shard_map(local, mesh=mesh, in_specs=in_specs, out_specs=out_specs, check_vma=False)
```
